32 devices in a mesh: tm: 4 (over y, x), pair: 8 (over z, core).
Axes of the slice: x: 2, y: 2, z: 4, core: 2. Of those that a mesh axis runs over, the one named last changes fastest.
Arguments:
- three_center: bfloat16 [192, 64, 1024], P('pair'), may hold values from -6 to 6
- green_occ: bfloat16 [4, 64, 64, 64], P('tm'), may hold values from -0.75 to 0.75
- green_vir: bfloat16 [4, 64, 64, 64], P('tm'), may hold values from -0.75 to 0.75
- pair_list: int32 [192], P('pair'), may hold values from 0 to 63
- block_counts: int32 [8], P('pair'), may hold values from 6 to 24, as said below
- cosine_weights: float32 [4, 4], replicated, may hold values from -3 to 3
- coulomb_rows: int32 [8, 3], replicated, may hold values from 0 to 7, as said below
- coulomb_blocks: float32 [8, 3, 128, 128], replicated, may hold values from -0.3125 to 0.3125
Outputs:
- screened: float32 [4, 1024, 1024], P('tm', 'pair')
The draws below stay inside these ranges and needn't reach their ends.
Inputs may be any that keep to these rules, and one draw needn't show every extreme that they name: `block_counts`: slots from the count on are not used; some index of pair has all 24 slots live. `coulomb_rows`: the row blocks of one column block are distinct, and the first is the column block itself.
All inputs are finite; a program needn't handle non-finite values.
Results may differ from the reference program's by a relative error of at most 0.0041.
Values sent between devices are 32-bit elements; how exact they have to be, the bound alone decides.
A program may use at most 64 MiB of HBM per device.

```python
import math
import jax
import jax.numpy as jnp
from jax import lax

PANEL = 1024
BW = 64
NGRP = 64
NB_DEV = 24
CB = 128
KPC = 3
NBLK = 192
TIMES = 4
FREQS = 4
NCOLB = 8
N_PAIR = 8


def draw_block_counts(key, part):
    count_key, full_key = jax.random.split(key)
    lowest = max(1, NB_DEV // 4)
    counts = jax.random.randint(count_key, (N_PAIR,), lowest, NB_DEV + 1)
    full_index = jax.random.randint(full_key, (), 0, N_PAIR)
    return counts.at[full_index].set(NB_DEV).astype(jnp.int32)


def draw_coulomb_rows(key, part):

    def single_column(column):
        shuffled = jax.random.permutation(jax.random.fold_in(key, column), NCOLB - 1)
        others = (column + 1 + shuffled[:KPC - 1]) % NCOLB
        return jnp.concatenate([column[None], others.astype(jnp.int32)])
    return jax.vmap(single_column)(jnp.arange(NCOLB, dtype=jnp.int32)).astype(jnp.int32)


def set_ends(array, stream_key, smallest, top_value):
    dims = array.shape
    place = [jax.random.randint(jax.random.fold_in(stream_key, axis), (), 0, dims[axis]) for axis in range(len(dims))]
    array = array.at[tuple(place)].set(smallest)
    longest = dims.index(max(dims))
    place[longest] = (place[longest] + 1) % dims[longest]
    return array.at[tuple(place)].set(top_value)


def with_spikes(result, key, source, target, blocks, factor):
    def block_of(axis_at):
        return (jnp.arange(result.shape[axis_at]) // (result.shape[axis_at] // blocks)).reshape((-1,) + (1,) * (result.ndim - 1 - axis_at))

    first = jax.random.permutation(key, blocks)[block_of(target)]
    other_side = (block_of(target) + blocks // 2) % blocks
    return jnp.where((block_of(source) == first) | (block_of(source) == other_side), factor * result, result)


def shard_levels(rng, shape, cuts, least, top_value):
    def one(axis_at, blocks):
        draws = jax.random.uniform(jax.random.fold_in(jax.random.fold_in(rng, 6), axis_at), (blocks,), jnp.float32, least / len(cuts), top_value / len(cuts))
        return jnp.repeat(jnp.exp(draws), shape[axis_at] // blocks).reshape((-1,) + (1,) * (len(shape) - axis_at - 1))

    factor_of = one(*cuts[0])
    for cut in cuts[1:]:
        factor_of = factor_of * one(*cut)
    return factor_of


def scatter_about(stream_key, shape, width, reach, cuts=(), kind=jnp.bfloat16):
    factor_of = shard_levels(stream_key, shape, cuts, -0.22, 0.18) if cuts else 1.0
    values = jax.random.normal(stream_key, shape, jnp.float32) * width * factor_of
    return jnp.minimum(jnp.maximum(values, -reach), reach).astype(kind)


def heavy_noise(stream_key, extent, width, limit, shards, heavy, kind=jnp.bfloat16):
    result = width * jax.random.normal(stream_key, extent, jnp.float32)
    if shards:
        result = result * shard_levels(stream_key, extent, shards, -0.22, 0.18)
    return jnp.clip(with_spikes(result, jax.random.fold_in(stream_key, 3), *heavy), -limit, limit).astype(kind)


def setup_inputs(seed: int = 0) -> dict:
    arg_keys = jax.random.split(jax.random.key(seed), 9)
    three_center = heavy_noise(arg_keys[0], (NBLK, BW, PANEL), 1.0, 6.0, ((0, 8),), (0, 2, 8, 2.0))
    green_occ = scatter_about(arg_keys[1], (TIMES, NGRP, BW, BW), BW ** -0.5, 0.75, ((0, 4),))
    green_vir = scatter_about(arg_keys[2], (TIMES, NGRP, BW, BW), BW ** -0.5, 0.75, ((0, 4),))
    pair_list = set_ends(jax.random.randint(arg_keys[3], (NBLK,), 0, NGRP), jax.random.fold_in(arg_keys[3], 1), 0, NGRP - 1).astype(jnp.int32)
    block_counts = draw_block_counts(jax.random.fold_in(arg_keys[8], 71), 0)
    cosine_weights = scatter_about(arg_keys[5], (FREQS, TIMES), TIMES ** -0.5, 3.0, (), jnp.float32)
    coulomb_rows = draw_coulomb_rows(jax.random.fold_in(arg_keys[8], 71), 0)
    coulomb_blocks = scatter_about(arg_keys[7], (NCOLB, KPC, CB, CB), (KPC * CB) ** -0.5, 0.3125, (), jnp.float32)
    return dict(three_center=three_center, green_occ=green_occ, green_vir=green_vir, pair_list=pair_list, block_counts=block_counts, cosine_weights=cosine_weights, coulomb_rows=coulomb_rows, coulomb_blocks=coulomb_blocks)


def reference(three_center, green_occ, green_vir, pair_list, block_counts, cosine_weights, coulomb_rows, coulomb_blocks):
    slot_index = jnp.arange(NBLK, dtype=jnp.int32)
    alive_mask = (slot_index % NB_DEV < block_counts[slot_index // NB_DEV]).astype(jnp.float32)
    expanded = three_center.astype(jnp.float32)
    normalizer = 1.0 / math.sqrt(NBLK * BW)

    def half_product(green_matrix):
        picked = green_matrix[pair_list].astype(jnp.float32)
        product = jnp.einsum('bij,bjp->bip', picked, expanded)
        product = product * alive_mask[:, None, None]
        return product.astype(jnp.bfloat16).reshape(NBLK * BW, PANEL)

    def single_time(greens):
        left_side = half_product(greens[0])
        right_side = half_product(greens[1])
        summed = lax.dot_general(left_side, right_side, (((0,), (0,)), ((), ())), preferred_element_type=jnp.float32)
        return summed * normalizer
    panels = lax.map(single_time, (green_occ, green_vir))
    spectra = jnp.einsum('ft,tpq->fpq', cosine_weights, panels, precision=lax.Precision.HIGHEST)
    blocked = spectra.reshape(FREQS * PANEL, NCOLB, CB)
    gathered = jnp.take(blocked, coulomb_rows.reshape(-1), axis=1)
    screened = jnp.einsum('mjx,jxy->mjy', gathered, coulomb_blocks.reshape(NCOLB * KPC, CB, CB), precision=lax.Precision.HIGHEST)
    return screened.reshape(FREQS * PANEL, NCOLB, KPC, CB).sum(axis=2).reshape(FREQS, PANEL, PANEL)
```

```python
import functools
import math

import jax
import jax.numpy as jnp
from jax import lax
from jax.experimental import pallas as pl
from jax.experimental.pallas import tpu as pltpu
from jax.sharding import PartitionSpec as P

MESH = pl.DeviceIdType.MESH
HOP_LAG = 2
CROSS_LAG = 2
CHUNK = 4


def slab_order(chips, pieces):
    order = []
    for z in range(chips):
        need = []
        for dest in range(chips):
            at = []
            if dest > z or (dest == z and z > 0):
                at.append(pieces * (chips - 1 - dest) + HOP_LAG * max(z - 1, 0))
            if dest < z or (dest == z and z < chips - 1):
                at.append(pieces * dest + HOP_LAG * max(chips - 2 - z, 0))
            need.append((min(at), dest))
        order.append([dest for _, dest in sorted(need)])
    return order


def half_product(green_matrix, pair_list, alive_mask, three_center):
    slots = pair_list.shape[0]
    picked = jnp.stack(
        [lax.dynamic_index_in_dim(green_matrix[0], pair_list[b], 0, False) for b in range(slots)]
    )
    product = jnp.einsum("bij,bjp->bip", picked, three_center, preferred_element_type=jnp.float32)
    product = product * alive_mask[:, None, None]
    return product.astype(jnp.bfloat16).reshape(-1, three_center.shape[2])


def collective_form(
    three_center,
    green_occ,
    green_vir,
    pair_list,
    block_counts,
    cosine_weights,
    coulomb_rows,
    coulomb_blocks,
):
    slots = three_center.shape[0]
    pair_devices = lax.axis_size("pair")
    alive_mask = (jnp.arange(slots, dtype=jnp.int32) < block_counts[0]).astype(jnp.float32)
    left_side = half_product(green_occ, pair_list, alive_mask, three_center)
    right_side = half_product(green_vir, pair_list, alive_mask, three_center)
    normalizer = 1.0 / math.sqrt(slots * three_center.shape[1] * pair_devices)
    summed = lax.dot_general(
        left_side, right_side, (((0,), (0,)), ((), ())), preferred_element_type=jnp.float32
    )
    row_slab = lax.psum_scatter(summed * normalizer, "pair", scatter_dimension=0, tiled=True)
    transformed = jnp.einsum(
        "ft,trc->frc",
        cosine_weights,
        lax.all_to_all(row_slab[None], "tm", split_axis=2, concat_axis=0, tiled=True),
        precision=lax.Precision.HIGHEST,
    )
    spectra = lax.all_to_all(transformed, "tm", split_axis=0, concat_axis=2, tiled=True)
    rows_here = spectra.shape[1]
    column_blocks = coulomb_rows.shape[0]
    per_column = coulomb_rows.shape[1]
    block_width = coulomb_blocks.shape[2]
    blocked = spectra.reshape(rows_here, column_blocks, block_width)
    picks = coulomb_rows.reshape(-1)
    gathered = jnp.stack(
        [
            lax.dynamic_index_in_dim(blocked, picks[j], 1, False)
            for j in range(column_blocks * per_column)
        ],
        axis=1,
    )
    factors = coulomb_blocks.reshape(column_blocks * per_column, block_width, block_width)
    screened = jnp.einsum("mjx,jxy->mjy", gathered, factors, precision=lax.Precision.HIGHEST)
    screened = screened.reshape(rows_here, column_blocks, per_column, block_width).sum(axis=2)
    return screened.reshape(1, rows_here, column_blocks * block_width)


def kernel(
    chips,
    normalizer,
    pair_list_ref,
    counts_ref,
    weights_ref,
    factor_rows_ref,
    three_hbm,
    occ_hbm,
    vir_hbm,
    coulomb_hbm,
    out_ref,
    three,
    occ,
    vir,
    factor,
    left,
    right,
    to_partner,
    from_partner,
    sums,
    arrived,
    x_in,
    y_out,
    y_in,
    mixed,
    spectra,
    coulomb_high,
    coulomb_low,
    three_sem,
    load_sem,
    partner_send,
    partner_recv,
    chain_send,
    chain_recv,
    cross_send,
    cross_recv,
):
    slots, width, panel = three.shape
    pieces, piece_rows = sums.shape[1], sums.shape[2]
    rows = pieces * piece_rows
    chunks = three_sem.shape[0]
    chunk = slots // chunks
    me = lax.axis_index("tm")
    place = lax.axis_index("pair")
    z = place // 2
    core = place % 2
    partner = z * 2 + 1 - core
    x_side = me + 1 - 2 * (me % 2)
    y_side = (me + 2) % 4
    y_side_x = (x_side + 2) % 4

    def three_copy(c):
        some = pl.ds(c * chunk, chunk)
        return pltpu.make_async_copy(three_hbm.at[some], three.at[some], three_sem.at[c])

    occ_copy = pltpu.make_async_copy(occ_hbm, occ, load_sem.at[0])
    vir_copy = pltpu.make_async_copy(vir_hbm, vir, load_sem.at[1])
    factor_copy = pltpu.make_async_copy(coulomb_hbm, factor, load_sem.at[2])
    occ_copy.start()
    vir_copy.start()
    for c in range(chunks):
        three_copy(c).start()
    factor_copy.start()

    barrier = pltpu.get_barrier_semaphore()
    pl.semaphore_signal(barrier, inc=1, device_id={"pair": partner}, device_id_type=MESH)
    pl.semaphore_signal(barrier, inc=1, device_id={"tm": x_side}, device_id_type=MESH)
    pl.semaphore_signal(barrier, inc=1, device_id={"tm": y_side}, device_id_type=MESH)

    @pl.when(z > 0)
    def _():
        pl.semaphore_signal(barrier, inc=1, device_id={"pair": place - 2}, device_id_type=MESH)

    @pl.when(z < chips - 1)
    def _():
        pl.semaphore_signal(barrier, inc=1, device_id={"pair": place + 2}, device_id_type=MESH)

    occ_copy.wait()
    vir_copy.wait()

    def half_step(c, carry):
        three_copy(c).wait()
        for k in range(chunk):
            slot = c * chunk + k
            group = pair_list_ref[slot]
            alive = (slot < counts_ref[0]).astype(jnp.float32)
            both = jnp.concatenate([occ[0, group], vir[0, group]], axis=0)
            product = jnp.dot(both, three[slot], preferred_element_type=jnp.float32) * alive
            product = product.astype(jnp.bfloat16)
            here = pl.ds(pl.multiple_of(slot * width, width), width)
            left[here, :] = product[:width]
            right[here, :] = product[width:]
        return carry

    lax.fori_loop(0, chunks, half_step, 0)

    neighbours = (z > 0).astype(jnp.int32) + (z < chips - 1).astype(jnp.int32)
    pl.semaphore_wait(barrier, 3 + neighbours)

    def panel_slab(slab):
        columns = pl.ds(pl.multiple_of(slab * rows, rows), rows)
        product = lax.dot_general(
            left[:, columns],
            right[...],
            (((0,), (0,)), ((), ())),
            preferred_element_type=jnp.float32,
        )
        return (product * normalizer).reshape(pieces, piece_rows, panel)

    def partner_copy(dest):
        return pltpu.make_async_remote_copy(
            src_ref=to_partner.at[dest],
            dst_ref=from_partner.at[dest],
            send_sem=partner_send.at[dest],
            recv_sem=partner_recv.at[dest],
            device_id={"pair": partner},
            device_id_type=MESH,
        )

    def chain_copy(way, dest, piece):
        return pltpu.make_async_remote_copy(
            src_ref=sums.at[dest, piece],
            dst_ref=arrived.at[way, dest, piece],
            send_sem=chain_send.at[dest, piece],
            recv_sem=chain_recv.at[way, dest, piece],
            device_id={"pair": place + 2 - 4 * way},
            device_id_type=MESH,
        )

    def x_copy(piece):
        return pltpu.make_async_remote_copy(
            src_ref=sums.at[z, piece],
            dst_ref=x_in.at[piece],
            send_sem=cross_send.at[0, piece],
            recv_sem=cross_recv.at[0, piece],
            device_id={"tm": x_side},
            device_id_type=MESH,
        )

    def y_copy(piece):
        return pltpu.make_async_remote_copy(
            src_ref=y_out.at[piece],
            dst_ref=y_in.at[piece],
            send_sem=cross_send.at[1, piece],
            recv_sem=cross_recv.at[1, piece],
            device_id={"tm": y_side},
            device_id_type=MESH,
        )

    order = slab_order(chips, pieces)

    def slab_at(step):
        dest = 0
        for row in range(chips):
            for k in range(chips):
                hit = jnp.logical_and(z == row, step == k).astype(jnp.int32)
                dest = dest + order[row][k] * hit
        return dest

    def start_slab(dest):
        to_partner[dest] = panel_slab(dest * 2 + 1 - core)
        partner_copy(dest).start()
        sums[dest] = panel_slab(dest * 2 + core)

    def finish_slab(dest):
        partner_copy(dest).wait_recv()

        def piece_step(piece, carry):
            sums[dest, piece] = sums[dest, piece] + from_partner[dest, piece]

            @pl.when(jnp.logical_and(z == 0, dest > z))
            def _():
                chain_copy(0, dest, piece).start()

            @pl.when(jnp.logical_and(z == chips - 1, dest < z))
            def _():
                chain_copy(1, dest, piece).start()

            return carry

        lax.fori_loop(0, pieces, piece_step, 0)

    def slab_step(step, carry):
        @pl.when(step < chips)
        def _():
            start_slab(slab_at(step))

        @pl.when(step > 0)
        def _():
            finish_slab(slab_at(step - 1))

        return carry

    lax.fori_loop(0, chips + 1, slab_step, 0)

    blocks, per_block, cb = factor.shape[0], factor.shape[1], factor.shape[2]
    factor_copy.wait()
    for block in range(blocks):
        exact = factor[block].reshape(per_block * cb, cb)
        high = exact.astype(jnp.bfloat16)
        coulomb_high[block] = high
        coulomb_low[block] = (exact - high.astype(jnp.float32)).astype(jnp.bfloat16)

    lag_up = HOP_LAG * jnp.maximum(z - 1, 0)
    lag_down = HOP_LAG * jnp.maximum(chips - 2 - z, 0)
    from_below = (z > 0).astype(jnp.int32) * (pieces * (chips - 1 - z) + lag_up)
    from_above = (z < chips - 1).astype(jnp.int32) * (pieces * z + lag_down)
    finish = jnp.maximum(from_below, from_above)

    def slot_step(slot, carry):
        for way in (0, 1):
            index = slot - (lag_down if way else lag_up)
            rank = index // pieces
            piece = index % pieces
            if way == 0:
                dest = chips - 1 - rank
                live = jnp.logical_and(z > 0, dest >= z)
                sends = dest > z
            else:
                dest = rank
                live = jnp.logical_and(z < chips - 1, dest <= z)
                sends = dest < z
            live = jnp.logical_and(index >= 0, live)

            @pl.when(live)
            def _():
                chain_copy(way, dest, piece).wait_recv()
                sums[dest, piece] = sums[dest, piece] + arrived[way, dest, piece]

                @pl.when(sends)
                def _():
                    chain_copy(way, dest, piece).start()

        done = slot - finish

        @pl.when(jnp.logical_and(done >= 0, done < pieces))
        def _():
            x_copy(done).start()

        crossed = done - CROSS_LAG

        @pl.when(jnp.logical_and(crossed >= 0, crossed < pieces))
        def _():
            x_copy(crossed).wait_recv()
            own = sums[z, crossed]
            other = x_in[crossed]
            y_out[crossed] = own * weights_ref[y_side, me] + other * weights_ref[y_side, x_side]
            y_copy(crossed).start()
            mixed[crossed] = own * weights_ref[me, me] + other * weights_ref[me, x_side]

        last = crossed - CROSS_LAG

        @pl.when(jnp.logical_and(last >= 0, last < pieces))
        def _():
            y_copy(last).wait_recv()
            whole = mixed[last] + y_in[last]
            at = pl.ds(pl.multiple_of(last * piece_rows, piece_rows), piece_rows)
            for block in range(blocks):
                spectra[block, at, :] = whole[:, block * cb : (block + 1) * cb]

        return carry

    most = max(
        max(pieces * (chips - 1 - at) + HOP_LAG * max(at - 1, 0) for at in range(1, chips)),
        max(pieces * at + HOP_LAG * max(chips - 2 - at, 0) for at in range(chips - 1)),
    )
    lax.fori_loop(0, most + pieces + 2 * CROSS_LAG, slot_step, 0)

    for block in range(blocks):
        gathered = jnp.concatenate(
            [spectra[factor_rows_ref[k, block]] for k in range(per_block)], axis=1
        )
        high = gathered.astype(jnp.bfloat16)
        low = (gathered - high.astype(jnp.float32)).astype(jnp.bfloat16)
        total = jnp.dot(high, coulomb_high[block], preferred_element_type=jnp.float32)
        total += jnp.dot(low, coulomb_high[block], preferred_element_type=jnp.float32)
        total += jnp.dot(high, coulomb_low[block], preferred_element_type=jnp.float32)
        out_ref[0, :, block * cb : (block + 1) * cb] = total

    def close_step(dest, carry):
        partner_copy(dest).wait_send()

        @pl.when(dest != z)
        def _():
            def close_piece(piece, inner):
                chain_copy(0, dest, piece).wait_send()
                return inner

            lax.fori_loop(0, pieces, close_piece, 0)

        return carry

    lax.fori_loop(0, chips, close_step, 0)

    def close_cross(piece, carry):
        x_copy(piece).wait_send()
        y_copy(piece).wait_send()
        return carry

    lax.fori_loop(0, pieces, close_cross, 0)


def kernel_form(
    pair_devices,
    three_center,
    green_occ,
    green_vir,
    pair_list,
    block_counts,
    cosine_weights,
    coulomb_rows,
    coulomb_blocks,
):
    slots, width, panel = three_center.shape
    chips = pair_devices // 2
    rows = panel // pair_devices
    pieces = max(1, rows // 16)
    piece_rows = rows // pieces
    blocks, per_block, cb, _ = coulomb_blocks.shape
    normalizer = 1.0 / math.sqrt(slots * width * pair_devices)
    smem = pl.BlockSpec(memory_space=pltpu.SMEM)
    vmem = pl.BlockSpec(memory_space=pltpu.VMEM)
    hbm = pl.BlockSpec(memory_space=pltpu.HBM)
    slab = (pieces, piece_rows, panel)
    chunks = slots // math.gcd(slots, CHUNK)
    return pl.pallas_call(
        functools.partial(kernel, chips, normalizer),
        out_shape=pltpu.VMEM((1, rows, panel), jnp.float32),
        in_specs=[smem] * 4 + [hbm] * 4,
        out_specs=vmem,
        scratch_shapes=[
            pltpu.VMEM(three_center.shape, jnp.bfloat16),
            pltpu.VMEM(green_occ.shape, jnp.bfloat16),
            pltpu.VMEM(green_vir.shape, jnp.bfloat16),
            pltpu.VMEM(coulomb_blocks.shape, jnp.float32),
            pltpu.VMEM((slots * width, panel), jnp.bfloat16),
            pltpu.VMEM((slots * width, panel), jnp.bfloat16),
            pltpu.VMEM((chips,) + slab, jnp.float32),
            pltpu.VMEM((chips,) + slab, jnp.float32),
            pltpu.VMEM((chips,) + slab, jnp.float32),
            pltpu.VMEM((2, chips) + slab, jnp.float32),
            pltpu.VMEM(slab, jnp.float32),
            pltpu.VMEM(slab, jnp.float32),
            pltpu.VMEM(slab, jnp.float32),
            pltpu.VMEM(slab, jnp.float32),
            pltpu.VMEM((blocks, rows, cb), jnp.float32),
            pltpu.VMEM((blocks, per_block * cb, cb), jnp.bfloat16),
            pltpu.VMEM((blocks, per_block * cb, cb), jnp.bfloat16),
            pltpu.SemaphoreType.DMA((chunks,)),
            pltpu.SemaphoreType.DMA((3,)),
            pltpu.SemaphoreType.DMA((chips,)),
            pltpu.SemaphoreType.DMA((chips,)),
            pltpu.SemaphoreType.DMA((chips, pieces)),
            pltpu.SemaphoreType.DMA((2, chips, pieces)),
            pltpu.SemaphoreType.DMA((2, pieces)),
            pltpu.SemaphoreType.DMA((2, pieces)),
        ],
        compiler_params=pltpu.CompilerParams(
            collective_id=0, has_side_effects=True, vmem_limit_bytes=60 * 1024 * 1024
        ),
    )(
        pair_list,
        block_counts,
        cosine_weights,
        coulomb_rows.T,
        three_center,
        green_occ,
        green_vir,
        coulomb_blocks,
    )


def solution(mesh):
    times, pair_devices = mesh.shape["tm"], mesh.shape["pair"]

    def local(*args):
        rows = args[0].shape[2] // pair_devices
        short = 4 <= pair_devices <= 16 and times == 4
        if short and pair_devices % 2 == 0 and rows % 128 == 0:
            return kernel_form(pair_devices, *args)
        return collective_form(*args)

    return jax.shard_map(
        local,
        mesh=mesh,
        in_specs=(
            P("pair", None, None),
            P("tm", None, None, None),
            P("tm", None, None, None),
            P("pair"),
            P("pair"),
            P(),
            P(),
            P(),
        ),
        out_specs=P("tm", "pair", None),
        check_vma=False,
    )
```

```python
import functools
import math

import jax
import jax.numpy as jnp
from jax import lax
from jax.experimental import pallas as pl
from jax.experimental.pallas import tpu as pltpu
from jax.sharding import PartitionSpec as P

MESH = pl.DeviceIdType.MESH
PIECE = 16
HOP_LAG = 4
CROSS_LAG = 3
CHUNK = 4
PARTS = 2


def slab_order(chips):
    order = []
    for z in range(chips):
        if z == 0:
            order.append(list(range(chips - 1, -1, -1)))
        elif z == chips - 1:
            order.append(list(range(chips)))
        else:
            up, down = chips - 1, 0
            ends = [up, down] if z < chips / 2 else [down, up]
            order.append(ends + [dest for dest in range(1, chips - 1)])
    return order


def half_product(green_matrix, pair_list, alive_mask, three_center):
    slots = pair_list.shape[0]
    picked = jnp.stack(
        [lax.dynamic_index_in_dim(green_matrix[0], pair_list[b], 0, False) for b in range(slots)]
    )
    product = jnp.einsum("bij,bjp->bip", picked, three_center, preferred_element_type=jnp.float32)
    product = product * alive_mask[:, None, None]
    return product.astype(jnp.bfloat16).reshape(-1, three_center.shape[2])


def collective_form(
    three_center,
    green_occ,
    green_vir,
    pair_list,
    block_counts,
    cosine_weights,
    coulomb_rows,
    coulomb_blocks,
):
    slots = three_center.shape[0]
    pair_devices = lax.axis_size("pair")
    alive_mask = (jnp.arange(slots, dtype=jnp.int32) < block_counts[0]).astype(jnp.float32)
    left_side = half_product(green_occ, pair_list, alive_mask, three_center)
    right_side = half_product(green_vir, pair_list, alive_mask, three_center)
    normalizer = 1.0 / math.sqrt(slots * three_center.shape[1] * pair_devices)
    summed = lax.dot_general(
        left_side, right_side, (((0,), (0,)), ((), ())), preferred_element_type=jnp.float32
    )
    row_slab = lax.psum_scatter(summed * normalizer, "pair", scatter_dimension=0, tiled=True)
    transformed = jnp.einsum(
        "ft,trc->frc",
        cosine_weights,
        lax.all_to_all(row_slab[None], "tm", split_axis=2, concat_axis=0, tiled=True),
        precision=lax.Precision.HIGHEST,
    )
    spectra = lax.all_to_all(transformed, "tm", split_axis=0, concat_axis=2, tiled=True)
    rows_here = spectra.shape[1]
    column_blocks = coulomb_rows.shape[0]
    per_column = coulomb_rows.shape[1]
    block_width = coulomb_blocks.shape[2]
    blocked = spectra.reshape(rows_here, column_blocks, block_width)
    picks = coulomb_rows.reshape(-1)
    gathered = jnp.stack(
        [
            lax.dynamic_index_in_dim(blocked, picks[j], 1, False)
            for j in range(column_blocks * per_column)
        ],
        axis=1,
    )
    factors = coulomb_blocks.reshape(column_blocks * per_column, block_width, block_width)
    screened = jnp.einsum("mjx,jxy->mjy", gathered, factors, precision=lax.Precision.HIGHEST)
    screened = screened.reshape(rows_here, column_blocks, per_column, block_width).sum(axis=2)
    return screened.reshape(1, rows_here, column_blocks * block_width)


def kernel(
    chips,
    normalizer,
    pair_list_ref,
    counts_ref,
    weights_ref,
    factor_rows_ref,
    three_hbm,
    occ_hbm,
    vir_hbm,
    coulomb_hbm,
    out_ref,
    three,
    occ,
    vir,
    factor,
    left,
    right,
    to_partner,
    from_partner,
    sums,
    arrived,
    x_in,
    y_out,
    y_in,
    mixed,
    spectra,
    coulomb_high,
    coulomb_low,
    three_sem,
    load_sem,
    partner_send,
    partner_recv,
    chain_send,
    chain_recv,
    cross_send,
    cross_recv,
):
    slots, width, panel = three.shape
    pieces, piece_rows = sums.shape[1], sums.shape[2]
    rows = pieces * piece_rows
    front = pieces // 2
    back = pieces - front
    middles = chips - 2
    items = middles * back
    chunks = three_sem.shape[0]
    chunk = slots // chunks
    blocks, per_block, cb = factor.shape[0], factor.shape[1], factor.shape[2]
    me = lax.axis_index("tm")
    place = lax.axis_index("pair")
    z = place // 2
    core = place % 2
    partner = z * 2 + 1 - core
    x_side = me + 1 - 2 * (me % 2)
    y_side = (me + 2) % 4
    is_end = jnp.logical_or(z == 0, z == chips - 1)

    def three_copy(c):
        some = pl.ds(c * chunk, chunk)
        return pltpu.make_async_copy(three_hbm.at[some], three.at[some], three_sem.at[c])

    occ_copy = pltpu.make_async_copy(occ_hbm, occ, load_sem.at[0])
    vir_copy = pltpu.make_async_copy(vir_hbm, vir, load_sem.at[1])
    factor_copy = pltpu.make_async_copy(coulomb_hbm, factor, load_sem.at[2])
    occ_copy.start()
    vir_copy.start()
    for c in range(chunks):
        three_copy(c).start()
    factor_copy.start()

    barrier = pltpu.get_barrier_semaphore()
    pl.semaphore_signal(barrier, inc=1, device_id={"pair": partner}, device_id_type=MESH)
    pl.semaphore_signal(barrier, inc=1, device_id={"tm": x_side}, device_id_type=MESH)
    pl.semaphore_signal(barrier, inc=1, device_id={"tm": y_side}, device_id_type=MESH)

    @pl.when(z > 0)
    def _():
        pl.semaphore_signal(barrier, inc=1, device_id={"pair": place - 2}, device_id_type=MESH)

    @pl.when(z < chips - 1)
    def _():
        pl.semaphore_signal(barrier, inc=1, device_id={"pair": place + 2}, device_id_type=MESH)

    order = slab_order(chips)

    def slab_at(step):
        dest = 0
        for row in range(chips):
            for k in range(chips):
                hit = jnp.logical_and(z == row, step == k).astype(jnp.int32)
                dest = dest + order[row][k] * hit
        return dest

    def panel_slab(slab, first, depth):
        columns = pl.ds(pl.multiple_of(slab * rows, rows), rows)
        some = pl.ds(first, depth)
        product = lax.dot_general(
            left[some, columns],
            right[some, :],
            (((0,), (0,)), ((), ())),
            preferred_element_type=jnp.float32,
        )
        return product.reshape(pieces, piece_rows, panel)

    occ_copy.wait()
    vir_copy.wait()
    head = slab_at(0)
    deep = chunk * width

    def half_step(c, carry):
        three_copy(c).wait()
        for k in range(chunk):
            slot = c * chunk + k
            group = pair_list_ref[slot]
            alive = (slot < counts_ref[0]).astype(jnp.float32)
            both = jnp.concatenate([occ[0, group], vir[0, group]], axis=0)
            product = jnp.dot(both, three[slot], preferred_element_type=jnp.float32) * alive
            product = product.astype(jnp.bfloat16)
            here = pl.ds(pl.multiple_of(slot * width, width), width)
            left[here, :] = product[:width]
            right[here, :] = product[width:]
        here = pl.multiple_of(c * deep, deep)

        @pl.when(c == 0)
        def _():
            to_partner[head] = panel_slab(head * 2 + 1 - core, here, deep)
            sums[head] = panel_slab(head * 2 + core, here, deep)

        @pl.when(c > 0)
        def _():
            to_partner[head] += panel_slab(head * 2 + 1 - core, here, deep)
            sums[head] += panel_slab(head * 2 + core, here, deep)

        return carry

    lax.fori_loop(0, chunks, half_step, 0)

    neighbours = (z > 0).astype(jnp.int32) + (z < chips - 1).astype(jnp.int32)
    pl.semaphore_wait(barrier, 3 + neighbours)

    def partner_copy(dest, part):
        some = pl.ds(part * (pieces // PARTS), pieces // PARTS)
        return pltpu.make_async_remote_copy(
            src_ref=to_partner.at[dest, some],
            dst_ref=from_partner.at[dest, some],
            send_sem=partner_send.at[dest, part],
            recv_sem=partner_recv.at[dest, part],
            device_id={"pair": partner},
            device_id_type=MESH,
        )

    def chain_copy(way, dest, piece):
        return pltpu.make_async_remote_copy(
            src_ref=sums.at[dest, piece],
            dst_ref=arrived.at[way, dest, piece],
            send_sem=chain_send.at[dest, piece],
            recv_sem=chain_recv.at[way, dest, piece],
            device_id={"pair": place + 2 - 4 * way},
            device_id_type=MESH,
        )

    def x_copy(dest, piece, at):
        return pltpu.make_async_remote_copy(
            src_ref=sums.at[dest, piece],
            dst_ref=x_in.at[at],
            send_sem=cross_send.at[0, at],
            recv_sem=cross_recv.at[0, at],
            device_id={"tm": x_side},
            device_id_type=MESH,
        )

    def y_copy(at):
        return pltpu.make_async_remote_copy(
            src_ref=y_out.at[at],
            dst_ref=y_in.at[at],
            send_sem=cross_send.at[1, at],
            recv_sem=cross_recv.at[1, at],
            device_id={"tm": y_side},
            device_id_type=MESH,
        )

    def end_send(dest, piece):
        @pl.when(jnp.logical_and(z == 0, dest > z))
        def _():
            chain_copy(0, dest, piece).start()

        @pl.when(jnp.logical_and(z == chips - 1, dest < z))
        def _():
            chain_copy(1, dest, piece).start()

    def partner_start(dest):
        for part in range(PARTS):
            partner_copy(dest, part).start()

    def finish_slab(dest):
        inner = jnp.logical_and(dest > 0, dest < chips - 1)
        for part in range(PARTS):
            partner_copy(dest, part).wait_recv()

            def piece_step(step, carry):
                piece = part * (pieces // PARTS) + step
                sums[dest, piece] = sums[dest, piece] + from_partner[dest, piece]

                @pl.when(jnp.logical_or(jnp.logical_not(inner), piece < front))
                def _():
                    end_send(dest, piece)

                return carry

            lax.fori_loop(0, pieces // PARTS, piece_step, 0)

    partner_start(head)

    def slab_step(step, carry):
        later = slab_at(step + 1)

        @pl.when(step + 1 < chips)
        def _():
            to_partner[later] = panel_slab(later * 2 + 1 - core, 0, slots * width)
            partner_start(later)

        finish_slab(slab_at(step))

        @pl.when(step + 1 < chips)
        def _():
            sums[later] = panel_slab(later * 2 + core, 0, slots * width)

        return carry

    lax.fori_loop(0, chips, slab_step, 0)

    factor_copy.wait()
    for block in range(blocks):
        exact = factor[block].reshape(per_block * cb, cb)
        high = exact.astype(jnp.bfloat16)
        coulomb_high[block] = high
        coulomb_low[block] = (exact - high.astype(jnp.float32)).astype(jnp.bfloat16)

    def apply_factor(held, store):
        for block in range(blocks):
            gathered = jnp.concatenate(
                [spectra[held, factor_rows_ref[k, block]] for k in range(per_block)], axis=1
            )
            high = gathered.astype(jnp.bfloat16)
            low = (gathered - high.astype(jnp.float32)).astype(jnp.bfloat16)
            total = jnp.dot(high, coulomb_high[block], preferred_element_type=jnp.float32)
            total += jnp.dot(low, coulomb_high[block], preferred_element_type=jnp.float32)
            total += jnp.dot(high, coulomb_low[block], preferred_element_type=jnp.float32)
            store(slice(block * cb, (block + 1) * cb), total)

    def cross_mix(dest, piece, at):
        x_copy(dest, piece, at).wait_recv()
        own = sums[dest, piece]
        other = x_in[at]

        def weight(f, t):
            return weights_ref[f, t] * normalizer

        y_out[at] = own * weight(y_side, me) + other * weight(y_side, x_side)
        y_copy(at).start()
        mixed[at] = own * weight(me, me) + other * weight(me, x_side)

    def cross_take(at, held, row):
        y_copy(at).wait_recv()
        whole = mixed[at] + y_in[at]
        here = pl.ds(pl.multiple_of(row * piece_rows, piece_rows), piece_rows)
        for block in range(blocks):
            spectra[held, block, here, :] = whole[:, block * cb : (block + 1) * cb]

    def item_place(item):
        rank = item // back
        dest = jnp.where(z < (chips + 1) // 2, chips - 2 - rank, 1 + rank)
        return dest, front + item % back

    lag_up = HOP_LAG * jnp.maximum(z - 1, 0)
    lag_down = HOP_LAG * jnp.maximum(chips - 2 - z, 0)

    def stream_slot(rank, piece):
        before = pieces + front * (rank - 1) + piece
        after = pieces + front * middles + back * (rank - 1) + piece - front
        return jnp.where(rank == 0, piece, jnp.where(piece < front, before, after))

    def both_ways(piece):
        below = jnp.where(z > 0, stream_slot(chips - 1 - z, piece) + lag_up, 0)
        above = jnp.where(z < chips - 1, stream_slot(z, piece) + lag_down, 0)
        return jnp.maximum(below, above)

    finish = both_ways(0)
    finish_back = both_ways(front)
    own_count = jnp.where(is_end, pieces, front)

    def slot_step(slot, carry):
        item = slot

        @pl.when(item < items)
        def _():
            dest, piece = item_place(item)
            x_copy(dest, piece, item).start()

        for way in (0, 1):
            index = slot - (lag_down if way else lag_up)
            over = index - pieces
            tail = over - front * middles
            rank = jnp.where(
                over < 0, 0, jnp.where(tail < 0, 1 + over // front, 1 + tail // back)
            )
            piece = jnp.where(
                over < 0, index, jnp.where(tail < 0, over % front, front + tail % back)
            )
            if way == 0:
                dest = chips - 1 - rank
                live = jnp.logical_and(z > 0, dest >= z)
                sends = dest > z
            else:
                dest = rank
                live = jnp.logical_and(z < chips - 1, dest <= z)
                sends = dest < z
            live = jnp.logical_and(jnp.logical_and(index >= 0, rank < chips), live)

            @pl.when(live)
            def _():
                chain_copy(way, dest, piece).wait_recv()
                sums[dest, piece] = sums[dest, piece] + arrived[way, dest, piece]

                @pl.when(sends)
                def _():
                    chain_copy(way, dest, piece).start()

        done = slot - finish

        @pl.when(jnp.logical_and(done >= 0, done < own_count))
        def _():
            x_copy(z, done, items + done).start()

        settled = slot - finish_back

        @pl.when(
            jnp.logical_and(jnp.logical_not(is_end), jnp.logical_and(settled >= 0, settled < back))
        )
        def _():
            at = pl.ds(pl.multiple_of((front + settled) * piece_rows, piece_rows), piece_rows)
            out_ref[0, at, :] = sums[z, front + settled]

        crossing = item - CROSS_LAG

        @pl.when(jnp.logical_and(crossing >= 0, crossing < items))
        def _():
            dest, piece = item_place(crossing)
            cross_mix(dest, piece, crossing)

        ready = crossing - CROSS_LAG

        @pl.when(jnp.logical_and(ready >= 0, ready < items))
        def _():
            dest, piece = item_place(ready)
            cross_take(ready, 0, piece - front)

            @pl.when(piece == pieces - 1)
            def _():
                for step in range(back):
                    x_copy(dest, front + step, ready - (back - 1) + step).wait_send()

                def store(columns, total):
                    sums[dest, front:, :, columns] = total.reshape(back, piece_rows, cb)

                apply_factor(0, store)
                for step in range(back):
                    end_send(dest, front + step)

        crossed = done - CROSS_LAG

        @pl.when(jnp.logical_and(crossed >= 0, crossed < own_count))
        def _():
            cross_mix(z, crossed, items + crossed)

        last = crossed - CROSS_LAG

        @pl.when(jnp.logical_and(last >= 0, last < own_count))
        def _():
            cross_take(items + last, 1, last % front)

            @pl.when(last % front == front - 1)
            def _():
                some = pl.ds(
                    pl.multiple_of((last // front) * front * piece_rows, front * piece_rows),
                    front * piece_rows,
                )

                def store(columns, total):
                    out_ref[0, some, columns] = total

                apply_factor(1, store)

        return carry

    end_most = pieces + HOP_LAG * middles + 2 * CROSS_LAG
    chain_most = pieces + front * middles + back * middles
    for at in range(1, chips - 1):
        up, down = HOP_LAG * (at - 1), HOP_LAG * (chips - 2 - at)
        first = max(front * (chips - 2 - at) + up, front * (at - 1) + down)
        final = max(back * (chips - 2 - at) + up, back * (at - 1) + down)
        end_most = max(end_most, pieces + first + front + 2 * CROSS_LAG)
        chain_most = max(chain_most, pieces + front * middles + final + back)
    lax.fori_loop(0, max(end_most, chain_most), slot_step, 0)

    def close_step(dest, carry):
        for part in range(PARTS):
            partner_copy(dest, part).wait_send()

        @pl.when(dest != z)
        def _():
            def close_piece(piece, inner):
                chain_copy(0, dest, piece).wait_send()
                return inner

            lax.fori_loop(0, pieces, close_piece, 0)

        return carry

    lax.fori_loop(0, chips, close_step, 0)

    def close_own(piece, carry):
        x_copy(z, piece, items + piece).wait_send()
        return carry

    lax.fori_loop(0, own_count, close_own, 0)

    def close_cross(at, carry):
        y_copy(at).wait_send()
        return carry

    lax.fori_loop(0, items + own_count, close_cross, 0)


def kernel_form(
    pair_devices,
    three_center,
    green_occ,
    green_vir,
    pair_list,
    block_counts,
    cosine_weights,
    coulomb_rows,
    coulomb_blocks,
):
    slots, width, panel = three_center.shape
    chips = pair_devices // 2
    rows = panel // pair_devices
    pieces = rows // PIECE
    piece_rows = rows // pieces
    blocks, per_block, cb, _ = coulomb_blocks.shape
    normalizer = 1.0 / math.sqrt(slots * width * pair_devices)
    smem = pl.BlockSpec(memory_space=pltpu.SMEM)
    vmem = pl.BlockSpec(memory_space=pltpu.VMEM)
    hbm = pl.BlockSpec(memory_space=pltpu.HBM)
    slab = (pieces, piece_rows, panel)
    across = (pieces + (chips - 2) * (pieces // 2), piece_rows, panel)
    chunks = slots // math.gcd(slots, CHUNK)
    return pl.pallas_call(
        functools.partial(kernel, chips, normalizer),
        out_shape=pltpu.VMEM((1, rows, panel), jnp.float32),
        in_specs=[smem] * 4 + [hbm] * 4,
        out_specs=vmem,
        scratch_shapes=[
            pltpu.VMEM(three_center.shape, jnp.bfloat16),
            pltpu.VMEM(green_occ.shape, jnp.bfloat16),
            pltpu.VMEM(green_vir.shape, jnp.bfloat16),
            pltpu.VMEM(coulomb_blocks.shape, jnp.float32),
            pltpu.VMEM((slots * width, panel), jnp.bfloat16),
            pltpu.VMEM((slots * width, panel), jnp.bfloat16),
            pltpu.VMEM((chips,) + slab, jnp.float32),
            pltpu.VMEM((chips,) + slab, jnp.float32),
            pltpu.VMEM((chips,) + slab, jnp.float32),
            pltpu.VMEM((2, chips) + slab, jnp.float32),
            pltpu.VMEM(across, jnp.float32),
            pltpu.VMEM(across, jnp.float32),
            pltpu.VMEM(across, jnp.float32),
            pltpu.VMEM(across, jnp.float32),
            pltpu.VMEM((2, blocks, rows // 2, cb), jnp.float32),
            pltpu.VMEM((blocks, per_block * cb, cb), jnp.bfloat16),
            pltpu.VMEM((blocks, per_block * cb, cb), jnp.bfloat16),
            pltpu.SemaphoreType.DMA((chunks,)),
            pltpu.SemaphoreType.DMA((3,)),
            pltpu.SemaphoreType.DMA((chips, PARTS)),
            pltpu.SemaphoreType.DMA((chips, PARTS)),
            pltpu.SemaphoreType.DMA((chips, pieces)),
            pltpu.SemaphoreType.DMA((2, chips, pieces)),
            pltpu.SemaphoreType.DMA((2, across[0])),
            pltpu.SemaphoreType.DMA((2, across[0])),
        ],
        compiler_params=pltpu.CompilerParams(
            collective_id=0, has_side_effects=True, vmem_limit_bytes=60 * 1024 * 1024
        ),
    )(
        pair_list,
        block_counts,
        cosine_weights,
        coulomb_rows.T,
        three_center,
        green_occ,
        green_vir,
        coulomb_blocks,
    )


def solution(mesh):
    times, pair_devices = mesh.shape["tm"], mesh.shape["pair"]

    def local(*args):
        rows = args[0].shape[2] // pair_devices
        short = 6 <= pair_devices <= 16 and times == 4
        if short and pair_devices % 2 == 0 and rows % 128 == 0:
            return kernel_form(pair_devices, *args)
        return collective_form(*args)

    return jax.shard_map(
        local,
        mesh=mesh,
        in_specs=(
            P("pair", None, None),
            P("tm", None, None, None),
            P("tm", None, None, None),
            P("pair"),
            P("pair"),
            P(),
            P(),
            P(),
        ),
        out_specs=P("tm", "pair", None),
        check_vma=False,
    )
```

```python
import functools
import math

import jax
import jax.numpy as jnp
from jax import lax
from jax.experimental import pallas as pl
from jax.experimental.pallas import tpu as pltpu
from jax.sharding import PartitionSpec as P

MESH = pl.DeviceIdType.MESH
HOP_LAG = 4
CROSS_LAG = 3
WORK = 2
END_WAIT = 2
MIDDLE_WAIT = 4


def slab_order(chips):
    order = []
    for z in range(chips):
        if z == 0:
            order.append(list(range(chips - 1, -1, -1)))
        elif z == chips - 1:
            order.append(list(range(chips)))
        else:
            inner = list(range(1, chips - 1))
            if z < chips / 2:
                order.append([chips - 1, 0] + inner[::-1])
            else:
                order.append([0, chips - 1] + inner)
    return order


def half_product(green_matrix, pair_list, alive_mask, three_center):
    slots = pair_list.shape[0]
    picked = jnp.stack(
        [lax.dynamic_index_in_dim(green_matrix[0], pair_list[b], 0, False) for b in range(slots)]
    )
    product = jnp.einsum("bij,bjp->bip", picked, three_center, preferred_element_type=jnp.float32)
    product = product * alive_mask[:, None, None]
    return product.astype(jnp.bfloat16).reshape(-1, three_center.shape[2])


def collective_form(
    three_center,
    green_occ,
    green_vir,
    pair_list,
    block_counts,
    cosine_weights,
    coulomb_rows,
    coulomb_blocks,
):
    slots = three_center.shape[0]
    pair_devices = lax.axis_size("pair")
    alive_mask = (jnp.arange(slots, dtype=jnp.int32) < block_counts[0]).astype(jnp.float32)
    left_side = half_product(green_occ, pair_list, alive_mask, three_center)
    right_side = half_product(green_vir, pair_list, alive_mask, three_center)
    normalizer = 1.0 / math.sqrt(slots * three_center.shape[1] * pair_devices)
    summed = lax.dot_general(
        left_side, right_side, (((0,), (0,)), ((), ())), preferred_element_type=jnp.float32
    )
    row_slab = lax.psum_scatter(summed * normalizer, "pair", scatter_dimension=0, tiled=True)
    transformed = jnp.einsum(
        "ft,trc->frc",
        cosine_weights,
        lax.all_to_all(row_slab[None], "tm", split_axis=2, concat_axis=0, tiled=True),
        precision=lax.Precision.HIGHEST,
    )
    spectra = lax.all_to_all(transformed, "tm", split_axis=0, concat_axis=2, tiled=True)
    rows_here = spectra.shape[1]
    column_blocks = coulomb_rows.shape[0]
    per_column = coulomb_rows.shape[1]
    block_width = coulomb_blocks.shape[2]
    blocked = spectra.reshape(rows_here, column_blocks, block_width)
    picks = coulomb_rows.reshape(-1)
    gathered = jnp.stack(
        [
            lax.dynamic_index_in_dim(blocked, picks[j], 1, False)
            for j in range(column_blocks * per_column)
        ],
        axis=1,
    )
    factors = coulomb_blocks.reshape(column_blocks * per_column, block_width, block_width)
    screened = jnp.einsum("mjx,jxy->mjy", gathered, factors, precision=lax.Precision.HIGHEST)
    screened = screened.reshape(rows_here, column_blocks, per_column, block_width).sum(axis=2)
    return screened.reshape(1, rows_here, column_blocks * block_width)


def kernel(
    chips,
    normalizer,
    pair_list_ref,
    counts_ref,
    weights_ref,
    factor_rows_ref,
    three_hbm,
    occ_hbm,
    vir_hbm,
    coulomb_hbm,
    out_ref,
    three,
    occ,
    vir,
    factor,
    left,
    right,
    from_partner,
    sums,
    arrived,
    x_in,
    y_out,
    y_in,
    mixed,
    spectra,
    coulomb_high,
    coulomb_low,
    three_sem,
    load_sem,
    partner_send,
    partner_recv,
    chain_send,
    chain_recv,
    cross_send,
    cross_recv,
):
    slots, width = three.shape[1], three.shape[2]
    half_rows, wide = sums.shape[4], sums.shape[5]
    pieces = 2 * chips
    middles = chips - 2
    items = middles * chips
    per_tile = wide // factor.shape[2]
    blocks, per_block, cb = factor.shape[0], factor.shape[1], factor.shape[2]
    me = lax.axis_index("tm")
    place = lax.axis_index("pair")
    z = place // 2
    core = place % 2
    partner = z * 2 + 1 - core
    x_side = me + 1 - 2 * (me % 2)
    y_side = (me + 2) % 4
    is_end = jnp.logical_or(z == 0, z == chips - 1)

    order = slab_order(chips)

    def slab_at(step):
        dest = 0
        for row in range(chips):
            for k in range(chips):
                hit = jnp.logical_and(z == row, step == k).astype(jnp.int32)
                dest = dest + order[row][k] * hit
        return dest

    head = slab_at(0)

    def three_copy(tile):
        columns = pl.ds(pl.multiple_of(tile * wide, wide), wide)
        return pltpu.make_async_copy(
            three_hbm.at[:, :, columns], three.at[tile], three_sem.at[tile]
        )

    occ_copy = pltpu.make_async_copy(occ_hbm, occ, load_sem.at[0])
    vir_copy = pltpu.make_async_copy(vir_hbm, vir, load_sem.at[1])
    factor_copy = pltpu.make_async_copy(coulomb_hbm, factor, load_sem.at[2])
    occ_copy.start()
    vir_copy.start()
    for step in range(chips):
        three_copy((head + step) % chips).start()
    factor_copy.start()

    barrier = pltpu.get_barrier_semaphore()
    pl.semaphore_signal(barrier, inc=1, device_id={"pair": partner}, device_id_type=MESH)
    pl.semaphore_signal(barrier, inc=1, device_id={"tm": x_side}, device_id_type=MESH)
    pl.semaphore_signal(barrier, inc=1, device_id={"tm": y_side}, device_id_type=MESH)

    @pl.when(z > 0)
    def _():
        pl.semaphore_signal(barrier, inc=1, device_id={"pair": place - 2}, device_id_type=MESH)

    @pl.when(z < chips - 1)
    def _():
        pl.semaphore_signal(barrier, inc=1, device_id={"pair": place + 2}, device_id_type=MESH)

    occ_copy.wait()
    vir_copy.wait()
    neighbours = (z > 0).astype(jnp.int32) + (z < chips - 1).astype(jnp.int32)

    def half_tile(tile):
        three_copy(tile).wait()
        for first in range(0, slots, 2):
            lefts = []
            for slot in (first, first + 1):
                group = pair_list_ref[slot]
                alive = (slot < counts_ref[0]).astype(jnp.bfloat16)
                both = jnp.concatenate([occ[0, group], vir[0, group]], axis=0) * alive
                product = jnp.dot(both, three[tile, slot], preferred_element_type=jnp.float32)
                product = product.astype(jnp.bfloat16)
                lefts.append(product[:width])
                right[tile, slot * width : (slot + 1) * width, :] = product[width:]
            left[tile, :, first * width : (first + 2) * width] = jnp.concatenate(lefts, axis=0).T

    def partner_copy(dest, tile):
        return pltpu.make_async_remote_copy(
            src_ref=sums.at[dest, 1 - core, tile],
            dst_ref=from_partner.at[dest, tile],
            send_sem=partner_send.at[dest, tile],
            recv_sem=partner_recv.at[dest, tile],
            device_id={"pair": partner},
            device_id_type=MESH,
        )

    def chain_copy(way, dest, tile, part):
        return pltpu.make_async_remote_copy(
            src_ref=sums.at[dest, core, tile, part],
            dst_ref=arrived.at[way, dest, tile, part],
            send_sem=chain_send.at[dest, tile, part],
            recv_sem=chain_recv.at[way, dest, tile, part],
            device_id={"pair": place + 2 - 4 * way},
            device_id_type=MESH,
        )

    def x_copy(dest, tile, part, at):
        return pltpu.make_async_remote_copy(
            src_ref=sums.at[dest, core, tile, part],
            dst_ref=x_in.at[at],
            send_sem=cross_send.at[0, at],
            recv_sem=cross_recv.at[0, at],
            device_id={"tm": x_side},
            device_id_type=MESH,
        )

    def y_copy(at):
        return pltpu.make_async_remote_copy(
            src_ref=y_out.at[at],
            dst_ref=y_in.at[at],
            send_sem=cross_send.at[1, at],
            recv_sem=cross_recv.at[1, at],
            device_id={"tm": y_side},
            device_id_type=MESH,
        )

    def end_send(dest, tile, part):
        @pl.when(jnp.logical_and(z == 0, dest > z))
        def _():
            chain_copy(0, dest, tile, part).start()

        @pl.when(jnp.logical_and(z == chips - 1, dest < z))
        def _():
            chain_copy(1, dest, tile, part).start()

    def step_place(step):
        dest = slab_at(step // chips)
        return dest, jnp.where(step < chips, (head + step) % chips, step % chips)

    early = z < (chips + 1) // 2

    def item_place(item):
        rank = item // chips
        return jnp.where(early, chips - 2 - rank, 1 + rank), item % chips

    def item_at(dest, tile):
        return jnp.where(early, chips - 2 - dest, dest - 1) * chips + tile

    def finish_step(step):
        dest, tile = step_place(step)
        inner = jnp.logical_and(dest > 0, dest < chips - 1)
        partner_copy(dest, tile).wait_recv()
        sums[dest, core, tile] = sums[dest, core, tile] + from_partner[dest, tile]
        end_send(dest, tile, 0)

        @pl.when(jnp.logical_not(inner))
        def _():
            end_send(dest, tile, 1)

        @pl.when(inner)
        def _():
            x_copy(dest, tile, 1, item_at(dest, tile)).start()

    def multiply_step(step):
        dest, tile = step_place(step)
        product = jnp.dot(left[dest], right[tile], preferred_element_type=jnp.float32)
        product = product.reshape(2, 2, half_rows, wide)
        sums[dest, 0, tile] = product[0]
        sums[dest, 1, tile] = product[1]

    def head_step(step, carry):
        half_tile((head + step) % chips)
        multiply_step(step)

        @pl.when(step == 0)
        def _():
            pl.semaphore_wait(barrier, 3 + neighbours)

        partner_copy(*step_place(step)).start()

        @pl.when(step > 0)
        def _():
            finish_step(step - 1)

        return carry

    lax.fori_loop(0, chips, head_step, 0)

    def split_factor():
        factor_copy.wait()
        for block in range(blocks):
            exact = factor[block].reshape(per_block * cb, cb)
            high = exact.astype(jnp.bfloat16)
            coulomb_high[block] = high
            coulomb_low[block] = (exact - high.astype(jnp.float32)).astype(jnp.bfloat16)

    def apply_factor(held, store):
        for block in range(blocks):
            gathered = jnp.concatenate(
                [spectra[held, factor_rows_ref[k, block]] for k in range(per_block)], axis=1
            )
            high = gathered.astype(jnp.bfloat16)
            low = (gathered - high.astype(jnp.float32)).astype(jnp.bfloat16)
            total = jnp.dot(high, coulomb_high[block], preferred_element_type=jnp.float32)
            total += jnp.dot(low, coulomb_high[block], preferred_element_type=jnp.float32)
            total += jnp.dot(high, coulomb_low[block], preferred_element_type=jnp.float32)
            store(block, total)

    def cross_mix(dest, tile, part, at):
        x_copy(dest, tile, part, at).wait_recv()
        own = sums[dest, core, tile, part]
        other = x_in[at]

        def weight(f, t):
            return weights_ref[f, t] * normalizer

        y_out[at] = own * weight(y_side, me) + other * weight(y_side, x_side)
        y_copy(at).start()
        mixed[at] = own * weight(me, me) + other * weight(me, x_side)

    def cross_take(at, held, tile):
        y_copy(at).wait_recv()
        whole = mixed[at] + y_in[at]
        for k in range(per_tile):
            spectra[held, tile * per_tile + k] = whole[:, k * cb : (k + 1) * cb]

    def end_piece(dest, piece):
        return (dest + piece // 2) % chips, piece % 2

    def own_place(piece):
        tile, part = end_piece(z, piece)
        return jnp.where(is_end, tile, piece), jnp.where(is_end, part, 0)

    lag_up = HOP_LAG * jnp.maximum(z - 1, 0)
    lag_down = HOP_LAG * jnp.maximum(chips - 2 - z, 0)

    def both_ways(part):
        def stream_slot(rank):
            inside = pieces + chips * (part * middles + rank - 1)
            return jnp.where(rank == 0, 0, inside)

        below = jnp.where(z > 0, stream_slot(chips - 1 - z) + lag_up, 0)
        above = jnp.where(z < chips - 1, stream_slot(z) + lag_down, 0)
        return jnp.maximum(below, above)

    finish = both_ways(0)
    finish_back = both_ways(1)
    own_count = jnp.where(is_end, pieces, chips)

    total = pieces + HOP_LAG * middles + 2 * CROSS_LAG
    total = max(total, pieces + 2 * items)
    for at in range(1, chips - 1):
        up, down = HOP_LAG * (at - 1), HOP_LAG * (chips - 2 - at)
        longest = max(chips * (chips - 1 - at) + up, chips * at + down)
        total = max(total, pieces + longest + 2 * CROSS_LAG)
        total = max(total, pieces + items + longest)

    def close():
        def close_step(dest, carry):
            def close_tile(tile, inner):
                partner_copy(dest, tile).wait_send()

                @pl.when(dest != z)
                def _():
                    for part in (0, 1):
                        chain_copy(0, dest, tile, part).wait_send()

                return inner

            lax.fori_loop(0, chips, close_tile, 0)
            return carry

        lax.fori_loop(0, chips, close_step, 0)

        def close_own(piece, carry):
            tile, part = own_place(piece)
            x_copy(z, tile, part, items + piece).wait_send()
            return carry

        lax.fori_loop(0, own_count, close_own, 0)

        def close_cross(at, carry):
            y_copy(at).wait_send()
            return carry

        lax.fori_loop(0, items + own_count, close_cross, 0)


    item_wait = jnp.where(is_end, END_WAIT, MIDDLE_WAIT)
    work_slots = chips * (chips - 1) // WORK

    def slot_step(slot, carry):
        for k in range(WORK):
            step = chips + WORK * slot + k

            @pl.when(step < chips * chips)
            def _():
                multiply_step(step)
                partner_copy(*step_place(step)).start()

        for k in range(WORK):
            step = chips - WORK + WORK * slot + k

            @pl.when(jnp.logical_and(step >= chips - 1, step < chips * chips))
            def _():
                finish_step(step)

        @pl.when(slot == work_slots)
        def _():
            split_factor()

        for way in (0, 1):
            index = slot - (lag_down if way else lag_up)
            over = index - pieces
            rank = jnp.where(over < 0, 0, 1 + (over // chips) % middles)
            dest = rank if way else chips - 1 - rank
            tile, part = end_piece(dest, index)
            tile = jnp.where(over < 0, tile, over % chips)
            part = jnp.where(over < 0, part, (over >= items).astype(jnp.int32))
            live = jnp.logical_and(index >= 0, over < 2 * items)
            if way == 0:
                live = jnp.logical_and(live, jnp.logical_and(z > 0, dest >= z))
                sends = dest > z
            else:
                live = jnp.logical_and(live, jnp.logical_and(z < chips - 1, dest <= z))
                sends = dest < z

            @pl.when(live)
            def _():
                chain_copy(way, dest, tile, part).wait_recv()
                sums[dest, core, tile, part] = (
                    sums[dest, core, tile, part] + arrived[way, dest, tile, part]
                )

                @pl.when(sends)
                def _():
                    chain_copy(way, dest, tile, part).start()

        done = slot - finish

        @pl.when(jnp.logical_and(done >= 0, done < own_count))
        def _():
            tile, part = own_place(done)
            x_copy(z, tile, part, items + done).start()

        settled = slot - finish_back

        @pl.when(
            jnp.logical_and(jnp.logical_not(is_end), jnp.logical_and(settled >= 0, settled < chips))
        )
        def _():
            columns = pl.ds(pl.multiple_of(settled * wide, wide), wide)
            out_ref[0, half_rows:, columns] = sums[z, core, settled, 1]

        crossing = slot - item_wait - CROSS_LAG

        @pl.when(jnp.logical_and(crossing >= 0, crossing < items))
        def _():
            dest, tile = item_place(crossing)
            cross_mix(dest, tile, 1, crossing)

        ready = crossing - CROSS_LAG

        @pl.when(jnp.logical_and(ready >= 0, ready < items))
        def _():
            dest, tile = item_place(ready)
            cross_take(ready, 0, tile)

            @pl.when(tile == chips - 1)
            def _():
                for step in range(chips):
                    x_copy(dest, step, 1, ready - (chips - 1) + step).wait_send()

                def store(block, total):
                    k = block % per_tile
                    sums[dest, core, block // per_tile, 1, :, k * cb : (k + 1) * cb] = total

                apply_factor(0, store)
                for step in range(chips):
                    end_send(dest, step, 1)

        crossed = done - CROSS_LAG

        @pl.when(jnp.logical_and(crossed >= 0, crossed < own_count))
        def _():
            tile, part = own_place(crossed)
            cross_mix(z, tile, part, items + crossed)

        last = crossed - CROSS_LAG

        @pl.when(jnp.logical_and(last >= 0, last < own_count))
        def _():
            tile, part = own_place(last)
            cross_take(items + last, 1 + part, tile)

            @pl.when(last >= own_count - jnp.where(is_end, 2, 1))
            def _():
                some = pl.ds(pl.multiple_of(part * half_rows, half_rows), half_rows)

                def store(block, total):
                    out_ref[0, some, block * cb : (block + 1) * cb] = total

                apply_factor(1 + part, store)

        @pl.when(jnp.logical_and(jnp.logical_not(is_end), slot == total - 2))
        def _():
            close()

        return carry

    lax.fori_loop(0, total, slot_step, 0)

    @pl.when(is_end)
    def _():
        close()


def kernel_form(
    pair_devices,
    three_center,
    green_occ,
    green_vir,
    pair_list,
    block_counts,
    cosine_weights,
    coulomb_rows,
    coulomb_blocks,
):
    slots, width, panel = three_center.shape
    chips = pair_devices // 2
    rows = panel // pair_devices
    wide = panel // chips
    piece = (rows // 2, wide)
    blocks, per_block, cb, _ = coulomb_blocks.shape
    normalizer = 1.0 / math.sqrt(slots * width * pair_devices)
    smem = pl.BlockSpec(memory_space=pltpu.SMEM)
    vmem = pl.BlockSpec(memory_space=pltpu.VMEM)
    hbm = pl.BlockSpec(memory_space=pltpu.HBM)
    across = 2 * chips + (chips - 2) * chips
    return pl.pallas_call(
        functools.partial(kernel, chips, normalizer),
        out_shape=pltpu.VMEM((1, rows, panel), jnp.float32),
        in_specs=[smem] * 4 + [hbm] * 4,
        out_specs=vmem,
        scratch_shapes=[
            pltpu.VMEM((chips, slots, width, wide), jnp.bfloat16),
            pltpu.VMEM(green_occ.shape, jnp.bfloat16),
            pltpu.VMEM(green_vir.shape, jnp.bfloat16),
            pltpu.VMEM(coulomb_blocks.shape, jnp.float32),
            pltpu.VMEM((chips, wide, slots * width), jnp.bfloat16),
            pltpu.VMEM((chips, slots * width, wide), jnp.bfloat16),
            pltpu.VMEM((chips, chips, 2) + piece, jnp.float32),
            pltpu.VMEM((chips, 2, chips, 2) + piece, jnp.float32),
            pltpu.VMEM((2, chips, chips, 2) + piece, jnp.float32),
            pltpu.VMEM((across,) + piece, jnp.float32),
            pltpu.VMEM((across,) + piece, jnp.float32),
            pltpu.VMEM((across,) + piece, jnp.float32),
            pltpu.VMEM((across,) + piece, jnp.float32),
            pltpu.VMEM((3, blocks, rows // 2, cb), jnp.float32),
            pltpu.VMEM((blocks, per_block * cb, cb), jnp.bfloat16),
            pltpu.VMEM((blocks, per_block * cb, cb), jnp.bfloat16),
            pltpu.SemaphoreType.DMA((chips,)),
            pltpu.SemaphoreType.DMA((3,)),
            pltpu.SemaphoreType.DMA((chips, chips)),
            pltpu.SemaphoreType.DMA((chips, chips)),
            pltpu.SemaphoreType.DMA((chips, chips, 2)),
            pltpu.SemaphoreType.DMA((2, chips, chips, 2)),
            pltpu.SemaphoreType.DMA((2, across)),
            pltpu.SemaphoreType.DMA((2, across)),
        ],
        compiler_params=pltpu.CompilerParams(
            collective_id=0, has_side_effects=True, vmem_limit_bytes=60 * 1024 * 1024
        ),
    )(
        pair_list,
        block_counts,
        cosine_weights,
        coulomb_rows.T,
        three_center,
        green_occ,
        green_vir,
        coulomb_blocks,
    )


def solution(mesh):
    times, pair_devices = mesh.shape["tm"], mesh.shape["pair"]

    def local(*args):
        slots, _, panel = args[0].shape
        cb = args[7].shape[2]
        short = 6 <= pair_devices <= 16 and pair_devices % 2 == 0 and times == 4
        fits = panel % (128 * pair_devices) == 0 and cb % 128 == 0 and slots % 2 == 0
        if short and fits and slots <= 32 and (2 * panel // pair_devices) % cb == 0:
            return kernel_form(pair_devices, *args)
        return collective_form(*args)

    return jax.shard_map(
        local,
        mesh=mesh,
        in_specs=(
            P("pair", None, None),
            P("tm", None, None, None),
            P("tm", None, None, None),
            P("pair"),
            P("pair"),
            P(),
            P(),
            P(),
        ),
        out_specs=P("tm", "pair", None),
        check_vma=False,
    )
```

```python
import functools
import math

import jax
import jax.numpy as jnp
from jax import lax
from jax.experimental import pallas as pl
from jax.experimental.pallas import tpu as pltpu
from jax.sharding import PartitionSpec as P

MESH = pl.DeviceIdType.MESH
HOP_LAG = 3
CROSS_LAG = 3
WORK = 2
END_WAIT = 1
MIDDLE_WAIT = 3


def slab_order(chips):
    order = []
    for z in range(chips):
        if z == 0:
            order.append(list(range(chips - 1, -1, -1)))
        elif z == chips - 1:
            order.append(list(range(chips)))
        else:
            inner = list(range(1, chips - 1))
            if z < chips / 2:
                order.append([chips - 1, 0] + inner[::-1])
            else:
                order.append([0, chips - 1] + inner)
    return order


def half_product(green_matrix, pair_list, alive_mask, three_center):
    slots = pair_list.shape[0]
    picked = jnp.stack(
        [lax.dynamic_index_in_dim(green_matrix[0], pair_list[b], 0, False) for b in range(slots)]
    )
    product = jnp.einsum("bij,bjp->bip", picked, three_center, preferred_element_type=jnp.float32)
    product = product * alive_mask[:, None, None]
    return product.astype(jnp.bfloat16).reshape(-1, three_center.shape[2])


def collective_form(
    three_center,
    green_occ,
    green_vir,
    pair_list,
    block_counts,
    cosine_weights,
    coulomb_rows,
    coulomb_blocks,
):
    slots = three_center.shape[0]
    pair_devices = lax.axis_size("pair")
    alive_mask = (jnp.arange(slots, dtype=jnp.int32) < block_counts[0]).astype(jnp.float32)
    left_side = half_product(green_occ, pair_list, alive_mask, three_center)
    right_side = half_product(green_vir, pair_list, alive_mask, three_center)
    normalizer = 1.0 / math.sqrt(slots * three_center.shape[1] * pair_devices)
    summed = lax.dot_general(
        left_side, right_side, (((0,), (0,)), ((), ())), preferred_element_type=jnp.float32
    )
    row_slab = lax.psum_scatter(summed * normalizer, "pair", scatter_dimension=0, tiled=True)
    transformed = jnp.einsum(
        "ft,trc->frc",
        cosine_weights,
        lax.all_to_all(row_slab[None], "tm", split_axis=2, concat_axis=0, tiled=True),
        precision=lax.Precision.HIGHEST,
    )
    spectra = lax.all_to_all(transformed, "tm", split_axis=0, concat_axis=2, tiled=True)
    rows_here = spectra.shape[1]
    column_blocks = coulomb_rows.shape[0]
    per_column = coulomb_rows.shape[1]
    block_width = coulomb_blocks.shape[2]
    blocked = spectra.reshape(rows_here, column_blocks, block_width)
    picks = coulomb_rows.reshape(-1)
    gathered = jnp.stack(
        [
            lax.dynamic_index_in_dim(blocked, picks[j], 1, False)
            for j in range(column_blocks * per_column)
        ],
        axis=1,
    )
    factors = coulomb_blocks.reshape(column_blocks * per_column, block_width, block_width)
    screened = jnp.einsum("mjx,jxy->mjy", gathered, factors, precision=lax.Precision.HIGHEST)
    screened = screened.reshape(rows_here, column_blocks, per_column, block_width).sum(axis=2)
    return screened.reshape(1, rows_here, column_blocks * block_width)


def kernel(
    chips,
    normalizer,
    pair_list_hbm,
    counts_hbm,
    weights_hbm,
    factor_rows_hbm,
    three_hbm,
    occ_hbm,
    vir_hbm,
    coulomb_hbm,
    out_ref,
    pair_list_ref,
    counts_ref,
    weights_ref,
    factor_rows_ref,
    three,
    occ,
    vir,
    factor,
    left,
    right,
    from_partner,
    sums,
    arrived,
    first_in,
    second_out,
    second_in,
    mixed,
    spectra,
    coulomb_high,
    coulomb_low,
    three_sem,
    load_sem,
    partner_send,
    partner_recv,
    chain_send,
    chain_recv,
    cross_send,
    cross_recv,
):
    slots, width = three.shape[1], three.shape[2]
    half_rows, wide = sums.shape[4], sums.shape[5]
    pieces = 2 * chips
    middles = chips - 2
    items = middles * chips
    per_tile = wide // factor.shape[2]
    blocks, per_block, cb = factor.shape[0], factor.shape[1], factor.shape[2]
    me = lax.axis_index("tm")
    place = lax.axis_index("pair")
    z = place // 2
    core = place % 2
    partner = z * 2 + 1 - core
    x_side = me + 1 - 2 * (me % 2)
    y_side = (me + 2) % 4

    def side(stage, at):
        return jnp.where((stage + at) % 2 == 0, x_side, y_side)

    is_end = jnp.logical_or(z == 0, z == chips - 1)

    barrier = pltpu.get_barrier_semaphore()
    pl.semaphore_signal(barrier, inc=1, device_id={"pair": partner}, device_id_type=MESH)
    pl.semaphore_signal(barrier, inc=1, device_id={"tm": x_side}, device_id_type=MESH)
    pl.semaphore_signal(barrier, inc=1, device_id={"tm": y_side}, device_id_type=MESH)

    @pl.when(z > 0)
    def _():
        pl.semaphore_signal(barrier, inc=1, device_id={"pair": place - 2}, device_id_type=MESH)

    @pl.when(z < chips - 1)
    def _():
        pl.semaphore_signal(barrier, inc=1, device_id={"pair": place + 2}, device_id_type=MESH)

    order = slab_order(chips)

    def slab_at(step):
        dest = 0
        for row in range(chips):
            for k in range(chips):
                hit = jnp.logical_and(z == row, step == k).astype(jnp.int32)
                dest = dest + order[row][k] * hit
        return dest

    head = slab_at(0)

    def three_copy(tile):
        columns = pl.ds(pl.multiple_of(tile * wide, wide), wide)
        return pltpu.make_async_copy(
            three_hbm.at[:, :, columns], three.at[tile], three_sem.at[tile]
        )

    occ_copy = pltpu.make_async_copy(occ_hbm, occ, load_sem.at[0])
    vir_copy = pltpu.make_async_copy(vir_hbm, vir, load_sem.at[1])
    factor_copy = pltpu.make_async_copy(coulomb_hbm, factor, load_sem.at[2])
    list_copy = pltpu.make_async_copy(pair_list_hbm, pair_list_ref, load_sem.at[3])
    counts_copy = pltpu.make_async_copy(counts_hbm, counts_ref, load_sem.at[4])
    weights_copy = pltpu.make_async_copy(weights_hbm, weights_ref, load_sem.at[5])
    rows_copy = pltpu.make_async_copy(factor_rows_hbm, factor_rows_ref, load_sem.at[6])
    list_copy.start()
    counts_copy.start()
    occ_copy.start()
    vir_copy.start()
    for step in range(chips):
        three_copy((head + step) % chips).start()
    weights_copy.start()
    rows_copy.start()
    factor_copy.start()

    list_copy.wait()
    counts_copy.wait()
    occ_copy.wait()
    vir_copy.wait()
    neighbours = (z > 0).astype(jnp.int32) + (z < chips - 1).astype(jnp.int32)

    def half_tile(tile):
        three_copy(tile).wait()
        for first in range(0, slots, 2):
            lefts = []
            for slot in (first, first + 1):
                group = pair_list_ref[slot]
                alive = (slot < counts_ref[0]).astype(jnp.bfloat16)
                both = jnp.concatenate([occ[0, group], vir[0, group]], axis=0) * alive
                product = jnp.dot(both, three[tile, slot], preferred_element_type=jnp.float32)
                product = product.astype(jnp.bfloat16)
                lefts.append(product[:width])
                right[tile, slot * width : (slot + 1) * width, :] = product[width:]
            left[tile, :, first * width : (first + 2) * width] = jnp.concatenate(lefts, axis=0).T

    def partner_copy(dest, tile, at):
        return pltpu.make_async_remote_copy(
            src_ref=sums.at[dest, 1 - core, tile],
            dst_ref=from_partner.at[dest, tile],
            send_sem=partner_send,
            recv_sem=partner_recv.at[at],
            device_id={"pair": partner},
            device_id_type=MESH,
        )

    def sent(bytes_of, send_sem):
        return pltpu.make_async_remote_copy(
            src_ref=bytes_of,
            dst_ref=bytes_of,
            send_sem=send_sem,
            recv_sem=partner_recv.at[0],
            device_id={"pair": partner},
            device_id_type=MESH,
        )

    def chain_copy(way, dest, tile, part):
        place_at = dest + 1 - way
        return pltpu.make_async_remote_copy(
            src_ref=sums.at[dest, core, tile, part],
            dst_ref=arrived.at[place_at, tile, part],
            send_sem=chain_send,
            recv_sem=chain_recv.at[place_at * pieces + part * chips + tile],
            device_id={"pair": place + 2 - 4 * way},
            device_id_type=MESH,
        )

    def cross_copy(source, target, stage, send_at, recv_at):
        return pltpu.make_async_remote_copy(
            src_ref=source,
            dst_ref=target,
            send_sem=cross_send.at[send_at],
            recv_sem=cross_recv.at[stage, recv_at],
            device_id={"tm": side(stage, recv_at)},
            device_id_type=MESH,
        )

    def first_item(dest, tile, item):
        source = sums.at[dest, core, tile, 1]
        return cross_copy(source, first_in.at[item], 0, item // chips, item)

    def second_copy(at):
        return cross_copy(second_out.at[at], second_in.at[at], 1, middles + 1, at)

    def first_own(tile, part, at):
        return cross_copy(sums.at[z, core, tile, part], first_in.at[at], 0, middles, at)

    def end_send(dest, tile, part):
        @pl.when(jnp.logical_and(z == 0, dest > z))
        def _():
            chain_copy(0, dest, tile, part).start()

        @pl.when(jnp.logical_and(z == chips - 1, dest < z))
        def _():
            chain_copy(1, dest, tile, part).start()

    def step_place(step):
        dest = slab_at(step // chips)
        return dest, jnp.where(step < chips, (head + step) % chips, step % chips)

    early = z < (chips + 1) // 2

    def item_place(item):
        rank = item // chips
        return jnp.where(early, chips - 2 - rank, 1 + rank), item % chips

    def item_at(dest, tile):
        return jnp.where(early, chips - 2 - dest, dest - 1) * chips + tile

    def head_tile(step):
        return (head + step) % chips

    def finish_head(step):
        tile = head_tile(step)
        partner_copy(head, tile, step).wait_recv()
        sums[head, core, tile] = sums[head, core, tile] + from_partner[head, tile]
        end_send(head, tile, 0)
        end_send(head, tile, 1)

    def finish_slab(at):
        dest = slab_at(at)
        inner = jnp.logical_and(dest > 0, dest < chips - 1)
        pltpu.make_async_remote_copy(
            src_ref=sums.at[dest, 1 - core],
            dst_ref=from_partner.at[dest],
            send_sem=partner_send,
            recv_sem=partner_recv.at[chips - 1 + at],
            device_id={"pair": partner},
            device_id_type=MESH,
        ).wait_recv()

        def tile_step(tile, carry):
            sums[dest, core, tile] = sums[dest, core, tile] + from_partner[dest, tile]

            @pl.when(inner)
            def _():
                end_send(dest, tile, 0)
                first_item(dest, tile, item_at(dest, tile)).start()

            return carry

        lax.fori_loop(0, chips, tile_step, 0)

    def multiply_step(step):
        dest, tile = step_place(step)
        product = jnp.dot(left[dest], right[tile], preferred_element_type=jnp.float32)
        product = product.reshape(2, 2, half_rows, wide)
        sums[dest, 0, tile] = product[0]
        sums[dest, 1, tile] = product[1]

    def head_step(step, carry):
        half_tile(head_tile(step))
        multiply_step(step)

        @pl.when(step == 0)
        def _():
            pl.semaphore_wait(barrier, 3 + neighbours)

        partner_copy(head, head_tile(step), step).start()

        @pl.when(step > 0)
        def _():
            finish_head(step - 1)

        return carry

    lax.fori_loop(0, chips, head_step, 0)
    finish_head(chips - 1)
    weights_copy.wait()
    rows_copy.wait()

    def split_factor():
        factor_copy.wait()
        for block in range(blocks):
            exact = factor[block].reshape(per_block * cb, cb)
            high = exact.astype(jnp.bfloat16)
            coulomb_high[block] = high
            coulomb_low[block] = (exact - high.astype(jnp.float32)).astype(jnp.bfloat16)

    def apply_factor(held, store):
        for block in range(blocks):
            gathered = jnp.concatenate(
                [spectra[held, factor_rows_ref[k, block]] for k in range(per_block)], axis=1
            )
            high = gathered.astype(jnp.bfloat16)
            low = (gathered - high.astype(jnp.float32)).astype(jnp.bfloat16)
            total = jnp.dot(high, coulomb_high[block], preferred_element_type=jnp.float32)
            total += jnp.dot(low, coulomb_high[block], preferred_element_type=jnp.float32)
            total += jnp.dot(high, coulomb_low[block], preferred_element_type=jnp.float32)
            store(block, total)

    def weight(f, t):
        return weights_ref[f, t] * normalizer

    def cross_mix(own, at):
        other = first_in[at]
        near, far = side(0, at), side(1, at)
        second_out[at] = own * weight(far, me) + other * weight(far, near)
        mixed[at] = own * weight(me, me) + other * weight(me, near)
        second_copy(at).start()

    def cross_take(whole, held, tile):
        for k in range(per_tile):
            spectra[held, tile * per_tile + k] = whole[:, k * cb : (k + 1) * cb]

    lag_up = HOP_LAG * jnp.maximum(z - 1, 0)
    lag_down = HOP_LAG * jnp.maximum(chips - 2 - z, 0)

    def both_ways(part):
        def stream_slot(rank):
            inside = pieces + chips * (part * middles + rank - 1)
            return jnp.where(rank == 0, 0, inside)

        below = jnp.where(z > 0, stream_slot(chips - 1 - z) + lag_up, 0)
        above = jnp.where(z < chips - 1, stream_slot(z) + lag_down, 0)
        return jnp.maximum(below, above)

    finish = both_ways(0)
    finish_back = both_ways(1)
    own_count = jnp.where(is_end, pieces, chips)

    total = pieces + HOP_LAG * middles + 2 * CROSS_LAG
    total = max(total, pieces + 2 * items)
    for at in range(1, chips - 1):
        up, down = HOP_LAG * (at - 1), HOP_LAG * (chips - 2 - at)
        longest = max(chips * (chips - 1 - at) + up, chips * at + down)
        total = max(total, pieces + longest + 2 * CROSS_LAG)
        total = max(total, pieces + items + longest)

    def close():
        sent(from_partner, partner_send).wait_send()
        sent(from_partner.at[pl.ds(0, chips - 1)], chain_send).wait_send()

        @pl.when(is_end)
        def _():
            sent(first_in.at[pl.ds(0, pieces)], cross_send.at[middles]).wait_send()
            sent(first_in.at[pl.ds(0, items + pieces)], cross_send.at[middles + 1]).wait_send()

        @pl.when(jnp.logical_not(is_end))
        def _():
            sent(first_in.at[pl.ds(0, chips)], cross_send.at[middles]).wait_send()
            sent(first_in.at[pl.ds(0, items + chips)], cross_send.at[middles + 1]).wait_send()

    item_wait = jnp.where(is_end, END_WAIT, MIDDLE_WAIT)
    work_slots = chips * (chips - 1) // WORK + 1

    def slot_step(slot, carry):
        for k in range(WORK):
            step = chips + WORK * slot + k

            @pl.when(step < chips * chips)
            def _():
                multiply_step(step)
                dest, tile = step_place(step)
                partner_copy(dest, tile, chips - 1 + step // chips).start()

        slab = slot * WORK // chips

        @pl.when(jnp.logical_and(slot * WORK % chips == 0, jnp.logical_and(slab > 0, slab < chips)))
        def _():
            finish_slab(slab)

        @pl.when(slot == work_slots)
        def _():
            split_factor()

        for way in (0, 1):
            index = slot - (lag_down if way else lag_up)
            comes = z < chips - 1 if way else z > 0
            first = 0 if way else chips - 1

            over = index - pieces
            rank = jnp.where(over < 0, 0, 1 + (over // chips) % middles)
            dest = rank if way else chips - 1 - rank
            tile = jnp.where(over < 0, (first + index // 2) % chips, over % chips)
            part = jnp.where(over < 0, index % 2, (over >= items).astype(jnp.int32))
            reaches = dest <= z if way else dest >= z
            sends = dest < z if way else dest > z
            live = jnp.logical_and(index >= 0, over < 2 * items)

            @pl.when(jnp.logical_and(jnp.logical_and(live, comes), reaches))
            def _():
                chain_copy(way, dest, tile, part).wait_recv()
                sums[dest, core, tile, part] = (
                    sums[dest, core, tile, part] + arrived[dest + 1 - way, tile, part]
                )

                @pl.when(sends)
                def _():
                    chain_copy(way, dest, tile, part).start()

        settled = slot - finish_back

        @pl.when(
            jnp.logical_and(jnp.logical_not(is_end), jnp.logical_and(settled >= 0, settled < chips))
        )
        def _():
            columns = pl.ds(pl.multiple_of(settled * wide, wide), wide)
            out_ref[0, half_rows:, columns] = sums[z, core, settled, 1]

        def own_stage(slots_ago, act):
            done = slot - finish - slots_ago

            @pl.when(jnp.logical_and(done >= 0, done < own_count))
            def _():
                tile = jnp.where(is_end, (z + done // 2) % chips, done)
                act(tile, jnp.where(is_end, done % 2, 0), items + done)

        def own_start(tile, part, at):
            first_own(tile, part, at).start()

        def own_mix(tile, part, at):
            first_own(tile, part, at).wait_recv()
            cross_mix(sums[z, core, tile, part], at)

        def own_take(tile, part, at):
            second_copy(at).wait_recv()
            cross_take(mixed[at] + second_in[at], 1 + part, tile)

            @pl.when(at - items >= own_count - jnp.where(is_end, 2, 1))
            def _():
                some = pl.ds(pl.multiple_of(part * half_rows, half_rows), half_rows)

                def store(block, total):
                    out_ref[0, some, block * cb : (block + 1) * cb] = total

                apply_factor(1 + part, store)

        own_stage(0, own_start)

        crossing = slot - item_wait - CROSS_LAG

        @pl.when(jnp.logical_and(crossing >= 0, crossing < items))
        def _():
            dest, tile = item_place(crossing)
            first_item(dest, tile, crossing).wait_recv()
            cross_mix(sums[dest, core, tile, 1], crossing)

        ready = crossing - CROSS_LAG

        @pl.when(jnp.logical_and(ready >= 0, ready < items))
        def _():
            dest, tile = item_place(ready)
            second_copy(ready).wait_recv()
            cross_take(mixed[ready] + second_in[ready], 0, tile)

            @pl.when(tile == chips - 1)
            def _():
                sent(first_in.at[pl.ds(0, chips)], cross_send.at[ready // chips]).wait_send()

                def store(block, total):
                    k = block % per_tile
                    sums[dest, core, block // per_tile, 1, :, k * cb : (k + 1) * cb] = total

                apply_factor(0, store)
                for step in range(chips):
                    end_send(dest, step, 1)

        own_stage(CROSS_LAG, own_mix)
        own_stage(2 * CROSS_LAG, own_take)

        @pl.when(jnp.logical_and(jnp.logical_not(is_end), slot == total - 2))
        def _():
            close()

        return carry

    lax.fori_loop(0, total, slot_step, 0)

    @pl.when(is_end)
    def _():
        close()


def kernel_form(
    pair_devices,
    three_center,
    green_occ,
    green_vir,
    pair_list,
    block_counts,
    cosine_weights,
    coulomb_rows,
    coulomb_blocks,
):
    slots, width, panel = three_center.shape
    chips = pair_devices // 2
    rows = panel // pair_devices
    wide = panel // chips
    piece = (rows // 2, wide)
    blocks, per_block, cb, _ = coulomb_blocks.shape
    normalizer = 1.0 / math.sqrt(slots * width * pair_devices)
    vmem = pl.BlockSpec(memory_space=pltpu.VMEM)
    hbm = pl.BlockSpec(memory_space=pltpu.HBM)
    across = 2 * chips + (chips - 2) * chips
    return pl.pallas_call(
        functools.partial(kernel, chips, normalizer),
        out_shape=pltpu.VMEM((1, rows, panel), jnp.float32),
        in_specs=[hbm] * 8,
        out_specs=vmem,
        scratch_shapes=[
            pltpu.SMEM(pair_list.shape, jnp.int32),
            pltpu.SMEM(block_counts.shape, jnp.int32),
            pltpu.SMEM(cosine_weights.shape, jnp.float32),
            pltpu.SMEM(coulomb_rows.shape[::-1], jnp.int32),
            pltpu.VMEM((chips, slots, width, wide), jnp.bfloat16),
            pltpu.VMEM(green_occ.shape, jnp.bfloat16),
            pltpu.VMEM(green_vir.shape, jnp.bfloat16),
            pltpu.VMEM(coulomb_blocks.shape, jnp.float32),
            pltpu.VMEM((chips, wide, slots * width), jnp.bfloat16),
            pltpu.VMEM((chips, slots * width, wide), jnp.bfloat16),
            pltpu.VMEM((chips, chips, 2) + piece, jnp.float32),
            pltpu.VMEM((chips, 2, chips, 2) + piece, jnp.float32),
            pltpu.VMEM((chips + 1, chips, 2) + piece, jnp.float32),
            pltpu.VMEM((across,) + piece, jnp.float32),
            pltpu.VMEM((across,) + piece, jnp.float32),
            pltpu.VMEM((across,) + piece, jnp.float32),
            pltpu.VMEM((across,) + piece, jnp.float32),
            pltpu.VMEM((3, blocks, rows // 2, cb), jnp.float32),
            pltpu.VMEM((blocks, per_block * cb, cb), jnp.bfloat16),
            pltpu.VMEM((blocks, per_block * cb, cb), jnp.bfloat16),
            pltpu.SemaphoreType.DMA((chips,)),
            pltpu.SemaphoreType.DMA((7,)),
            pltpu.SemaphoreType.DMA,
            pltpu.SemaphoreType.DMA((2 * chips - 1,)),
            pltpu.SemaphoreType.DMA,
            pltpu.SemaphoreType.DMA(((chips + 1) * 2 * chips,)),
            pltpu.SemaphoreType.DMA((chips,)),
            pltpu.SemaphoreType.DMA((2, across)),
        ],
        compiler_params=pltpu.CompilerParams(
            collective_id=0, has_side_effects=True, vmem_limit_bytes=60 * 1024 * 1024
        ),
    )(
        pair_list,
        block_counts,
        cosine_weights,
        coulomb_rows.T,
        three_center,
        green_occ,
        green_vir,
        coulomb_blocks,
    )


def solution(mesh):
    times, pair_devices = mesh.shape["tm"], mesh.shape["pair"]

    def local(*args):
        slots, _, panel = args[0].shape
        cb = args[7].shape[2]
        short = 6 <= pair_devices <= 16 and pair_devices % 2 == 0 and times == 4
        fits = panel % (128 * pair_devices) == 0 and cb % 128 == 0 and slots % 2 == 0
        if short and fits and slots <= 32 and (2 * panel // pair_devices) % cb == 0:
            return kernel_form(pair_devices, *args)
        return collective_form(*args)

    return jax.shard_map(
        local,
        mesh=mesh,
        in_specs=(
            P("pair", None, None),
            P("tm", None, None, None),
            P("tm", None, None, None),
            P("pair"),
            P("pair"),
            P(),
            P(),
            P(),
        ),
        out_specs=P("tm", "pair", None),
        check_vma=False,
    )
```

```python
import functools
import math

import jax
import jax.numpy as jnp
from jax import lax
from jax.experimental import pallas as pl
from jax.experimental.pallas import tpu as pltpu
from jax.sharding import PartitionSpec as P

MESH = pl.DeviceIdType.MESH
HOP_LAG = 3
CROSS_LAG = 3
WORK = 2
END_WAIT = 1
MIDDLE_WAIT = 3


def slab_order(chips):
    order = []
    for z in range(chips):
        if z == 0:
            order.append(list(range(chips - 1, -1, -1)))
        elif z == chips - 1:
            order.append(list(range(chips)))
        else:
            inner = list(range(1, chips - 1))
            if z < chips / 2:
                order.append([chips - 1, 0] + inner[::-1])
            else:
                order.append([0, chips - 1] + inner)
    return order


def half_product(green_matrix, pair_list, alive_mask, three_center):
    slots = pair_list.shape[0]
    picked = jnp.stack(
        [lax.dynamic_index_in_dim(green_matrix[0], pair_list[b], 0, False) for b in range(slots)]
    )
    product = jnp.einsum("bij,bjp->bip", picked, three_center, preferred_element_type=jnp.float32)
    product = product * alive_mask[:, None, None]
    return product.astype(jnp.bfloat16).reshape(-1, three_center.shape[2])


def collective_form(
    three_center,
    green_occ,
    green_vir,
    pair_list,
    block_counts,
    cosine_weights,
    coulomb_rows,
    coulomb_blocks,
):
    slots = three_center.shape[0]
    pair_devices = lax.axis_size("pair")
    alive_mask = (jnp.arange(slots, dtype=jnp.int32) < block_counts[0]).astype(jnp.float32)
    left_side = half_product(green_occ, pair_list, alive_mask, three_center)
    right_side = half_product(green_vir, pair_list, alive_mask, three_center)
    normalizer = 1.0 / math.sqrt(slots * three_center.shape[1] * pair_devices)
    summed = lax.dot_general(
        left_side, right_side, (((0,), (0,)), ((), ())), preferred_element_type=jnp.float32
    )
    row_slab = lax.psum_scatter(summed * normalizer, "pair", scatter_dimension=0, tiled=True)
    transformed = jnp.einsum(
        "ft,trc->frc",
        cosine_weights,
        lax.all_to_all(row_slab[None], "tm", split_axis=2, concat_axis=0, tiled=True),
        precision=lax.Precision.HIGHEST,
    )
    spectra = lax.all_to_all(transformed, "tm", split_axis=0, concat_axis=2, tiled=True)
    rows_here = spectra.shape[1]
    column_blocks = coulomb_rows.shape[0]
    per_column = coulomb_rows.shape[1]
    block_width = coulomb_blocks.shape[2]
    blocked = spectra.reshape(rows_here, column_blocks, block_width)
    picks = coulomb_rows.reshape(-1)
    gathered = jnp.stack(
        [
            lax.dynamic_index_in_dim(blocked, picks[j], 1, False)
            for j in range(column_blocks * per_column)
        ],
        axis=1,
    )
    factors = coulomb_blocks.reshape(column_blocks * per_column, block_width, block_width)
    screened = jnp.einsum("mjx,jxy->mjy", gathered, factors, precision=lax.Precision.HIGHEST)
    screened = screened.reshape(rows_here, column_blocks, per_column, block_width).sum(axis=2)
    return screened.reshape(1, rows_here, column_blocks * block_width)


def kernel(
    chips,
    normalizer,
    pair_list_hbm,
    counts_hbm,
    weights_hbm,
    factor_rows_hbm,
    three_hbm,
    occ_hbm,
    vir_hbm,
    coulomb_hbm,
    out_ref,
    pair_list_ref,
    counts_ref,
    weights_ref,
    factor_rows_ref,
    three,
    occ,
    vir,
    factor,
    left,
    right,
    from_partner,
    sums,
    arrived,
    raw_out,
    raw_in,
    first_in,
    second_out,
    second_in,
    mixed,
    spectra,
    coulomb_high,
    coulomb_low,
    three_sem,
    load_sem,
    partner_send,
    partner_recv,
    chain_send,
    chain_recv,
    raw_send,
    raw_recv,
    cross_send,
    cross_recv,
):
    slots, width = three.shape[1], three.shape[2]
    half_rows, wide = sums.shape[4], sums.shape[5]
    pieces = 2 * chips
    middles = chips - 2
    items = middles * chips
    per_tile = wide // factor.shape[2]
    blocks, per_block, cb = factor.shape[0], factor.shape[1], factor.shape[2]
    me = lax.axis_index("tm")
    place = lax.axis_index("pair")
    z = place // 2
    core = place % 2
    partner = z * 2 + 1 - core
    x_side = me + 1 - 2 * (me % 2)
    y_side = (me + 2) % 4

    def side(stage, at):
        return jnp.where((stage + at) % 2 == 0, x_side, y_side)

    is_end = jnp.logical_or(z == 0, z == chips - 1)

    barrier = pltpu.get_barrier_semaphore()
    pl.semaphore_signal(barrier, inc=1, device_id={"pair": partner}, device_id_type=MESH)
    pl.semaphore_signal(barrier, inc=1, device_id={"tm": x_side}, device_id_type=MESH)
    pl.semaphore_signal(barrier, inc=1, device_id={"tm": y_side}, device_id_type=MESH)

    @pl.when(z > 0)
    def _():
        pl.semaphore_signal(barrier, inc=1, device_id={"pair": place - 2}, device_id_type=MESH)

    @pl.when(z < chips - 1)
    def _():
        pl.semaphore_signal(barrier, inc=1, device_id={"pair": place + 2}, device_id_type=MESH)

    for here, there in ((0, 1), (1, 0), (chips - 1, chips - 2), (chips - 2, chips - 1)):

        @pl.when(z == here)
        def _():
            pl.semaphore_signal(
                barrier, inc=1, device_id={"pair": there * 2 + 1 - core}, device_id_type=MESH
            )

    order = slab_order(chips)

    def slab_at(step):
        dest = 0
        for row in range(chips):
            for k in range(chips):
                hit = jnp.logical_and(z == row, step == k).astype(jnp.int32)
                dest = dest + order[row][k] * hit
        return dest

    head = slab_at(0)

    def three_copy(tile):
        columns = pl.ds(pl.multiple_of(tile * wide, wide), wide)
        return pltpu.make_async_copy(
            three_hbm.at[:, :, columns], three.at[tile], three_sem.at[tile]
        )

    occ_copy = pltpu.make_async_copy(occ_hbm, occ, load_sem.at[0])
    vir_copy = pltpu.make_async_copy(vir_hbm, vir, load_sem.at[1])
    factor_copy = pltpu.make_async_copy(coulomb_hbm, factor, load_sem.at[2])
    list_copy = pltpu.make_async_copy(pair_list_hbm, pair_list_ref, load_sem.at[3])
    counts_copy = pltpu.make_async_copy(counts_hbm, counts_ref, load_sem.at[4])
    weights_copy = pltpu.make_async_copy(weights_hbm, weights_ref, load_sem.at[5])
    rows_copy = pltpu.make_async_copy(factor_rows_hbm, factor_rows_ref, load_sem.at[6])
    list_copy.start()
    counts_copy.start()
    occ_copy.start()
    vir_copy.start()
    for step in range(chips):
        three_copy((head + step) % chips).start()
    weights_copy.start()
    rows_copy.start()
    factor_copy.start()

    list_copy.wait()
    counts_copy.wait()
    occ_copy.wait()
    vir_copy.wait()
    neighbours = (z > 0).astype(jnp.int32) + (z < chips - 1).astype(jnp.int32)
    for here in (0, 1, chips - 2, chips - 1):
        neighbours = neighbours + (z == here).astype(jnp.int32)

    def half_tile(tile):
        three_copy(tile).wait()
        for first in range(0, slots, 2):
            lefts = []
            for slot in (first, first + 1):
                group = pair_list_ref[slot]
                alive = (slot < counts_ref[0]).astype(jnp.bfloat16)
                both = jnp.concatenate([occ[0, group], vir[0, group]], axis=0) * alive
                product = jnp.dot(both, three[tile, slot], preferred_element_type=jnp.float32)
                product = product.astype(jnp.bfloat16)
                lefts.append(product[:width])
                right[tile, slot * width : (slot + 1) * width, :] = product[width:]
            left[tile, :, first * width : (first + 2) * width] = jnp.concatenate(lefts, axis=0).T

    def partner_copy(dest, tile, at):
        return pltpu.make_async_remote_copy(
            src_ref=sums.at[dest, 1 - core, tile],
            dst_ref=from_partner.at[dest, tile],
            send_sem=partner_send,
            recv_sem=partner_recv.at[at],
            device_id={"pair": partner},
            device_id_type=MESH,
        )

    def sent(bytes_of, send_sem):
        return pltpu.make_async_remote_copy(
            src_ref=bytes_of,
            dst_ref=bytes_of,
            send_sem=send_sem,
            recv_sem=partner_recv.at[0],
            device_id={"pair": partner},
            device_id_type=MESH,
        )

    def chain_copy(way, dest, tile, part, rows=slice(None)):
        place_at = dest + 1 - way
        rows = pl.ds(rows.start or 0, half_rows - (rows.start or 0))
        return pltpu.make_async_remote_copy(
            src_ref=sums.at[dest, core, tile, part, rows],
            dst_ref=arrived.at[place_at, tile, part, rows],
            send_sem=chain_send,
            recv_sem=chain_recv.at[place_at * pieces + part * chips + tile],
            device_id={"pair": place + 2 - 4 * way},
            device_id_type=MESH,
        )

    raw_rows = raw_in.shape[1]
    rest = slice(raw_rows, None)

    def raw_copy(across):
        there = jnp.where(z == 0, 1, chips - 2) * 2 + (1 - core if across else core)
        return pltpu.make_async_remote_copy(
            src_ref=raw_out.at[across],
            dst_ref=raw_in.at[across],
            send_sem=raw_send if across else chain_send,
            recv_sem=raw_recv.at[across],
            device_id={"pair": there},
            device_id_type=MESH,
        )

    def cross_copy(source, target, stage, send_at, recv_at):
        return pltpu.make_async_remote_copy(
            src_ref=source,
            dst_ref=target,
            send_sem=cross_send.at[send_at],
            recv_sem=cross_recv.at[stage, recv_at],
            device_id={"tm": side(stage, recv_at)},
            device_id_type=MESH,
        )

    def first_item(dest, tile, item):
        source = sums.at[dest, core, tile, 1]
        return cross_copy(source, first_in.at[item], 0, item // chips, item)

    def second_copy(at):
        return cross_copy(second_out.at[at], second_in.at[at], 1, middles + 1, at)

    def first_own(tile, part, at):
        return cross_copy(sums.at[z, core, tile, part], first_in.at[at], 0, middles, at)

    def end_send(dest, tile, part, rows=slice(None)):
        @pl.when(jnp.logical_and(z == 0, dest > z))
        def _():
            chain_copy(0, dest, tile, part, rows).start()

        @pl.when(jnp.logical_and(z == chips - 1, dest < z))
        def _():
            chain_copy(1, dest, tile, part, rows).start()

    def step_place(step):
        dest = slab_at(step // chips)
        return dest, jnp.where(step < chips, (head + step) % chips, step % chips)

    early = z < (chips + 1) // 2

    def item_place(item):
        rank = item // chips
        return jnp.where(early, chips - 2 - rank, 1 + rank), item % chips

    def item_at(dest, tile):
        return jnp.where(early, chips - 2 - dest, dest - 1) * chips + tile

    def head_tile(step):
        return (head + step) % chips

    def finish_head(step):
        tile = head_tile(step)
        partner_copy(head, tile, step).wait_recv()
        sums[head, core, tile] = sums[head, core, tile] + from_partner[head, tile]

        @pl.when(step == 0)
        def _():
            end_send(head, tile, 0, rest)

        @pl.when(step > 0)
        def _():
            end_send(head, tile, 0)

        end_send(head, tile, 1)

    def finish_slab(at):
        dest = slab_at(at)
        inner = jnp.logical_and(dest > 0, dest < chips - 1)
        pltpu.make_async_remote_copy(
            src_ref=sums.at[dest, 1 - core],
            dst_ref=from_partner.at[dest],
            send_sem=partner_send,
            recv_sem=partner_recv.at[chips - 1 + at],
            device_id={"pair": partner},
            device_id_type=MESH,
        ).wait_recv()

        def tile_step(tile, carry):
            sums[dest, core, tile] = sums[dest, core, tile] + from_partner[dest, tile]

            @pl.when(inner)
            def _():
                end_send(dest, tile, 0)
                first_item(dest, tile, item_at(dest, tile)).start()

            return carry

        lax.fori_loop(0, chips, tile_step, 0)

    def multiply_step(step):
        dest, tile = step_place(step)
        product = jnp.dot(left[dest], right[tile], preferred_element_type=jnp.float32)
        product = product.reshape(2, 2, half_rows, wide)
        sums[dest, 0, tile] = product[0]
        sums[dest, 1, tile] = product[1]

    def head_step(step, carry):
        half_tile(head_tile(step))
        multiply_step(step)

        @pl.when(step == 0)
        def _():
            pl.semaphore_wait(barrier, 3 + neighbours)

        partner_copy(head, head_tile(step), step).start()

        @pl.when(jnp.logical_and(is_end, step == 0))
        def _():
            raw_out[0] = sums[head, core, head, 0, :raw_rows]
            raw_out[1] = sums[head, 1 - core, head, 0, :raw_rows]
            raw_copy(0).start()
            raw_copy(1).start()

        @pl.when(step > 0)
        def _():
            finish_head(step - 1)

        return carry

    lax.fori_loop(0, chips, head_step, 0)
    finish_head(chips - 1)
    weights_copy.wait()
    rows_copy.wait()

    def split_factor():
        factor_copy.wait()
        for block in range(blocks):
            exact = factor[block].reshape(per_block * cb, cb)
            high = exact.astype(jnp.bfloat16)
            coulomb_high[block] = high
            coulomb_low[block] = (exact - high.astype(jnp.float32)).astype(jnp.bfloat16)

    def apply_factor(held, store):
        for block in range(blocks):
            gathered = jnp.concatenate(
                [spectra[held, factor_rows_ref[k, block]] for k in range(per_block)], axis=1
            )
            high = gathered.astype(jnp.bfloat16)
            low = (gathered - high.astype(jnp.float32)).astype(jnp.bfloat16)
            total = jnp.dot(high, coulomb_high[block], preferred_element_type=jnp.float32)
            total += jnp.dot(low, coulomb_high[block], preferred_element_type=jnp.float32)
            total += jnp.dot(high, coulomb_low[block], preferred_element_type=jnp.float32)
            store(block, total)

    def weight(f, t):
        return weights_ref[f, t] * normalizer

    def cross_mix(own, at):
        other = first_in[at]
        near, far = side(0, at), side(1, at)
        second_out[at] = own * weight(far, me) + other * weight(far, near)
        mixed[at] = own * weight(me, me) + other * weight(me, near)
        second_copy(at).start()

    def cross_take(whole, held, tile):
        for k in range(per_tile):
            spectra[held, tile * per_tile + k] = whole[:, k * cb : (k + 1) * cb]

    lag_up = HOP_LAG * jnp.maximum(z - 1, 0)
    lag_down = HOP_LAG * jnp.maximum(chips - 2 - z, 0)

    def both_ways(part):
        def stream_slot(rank):
            inside = pieces + chips * (part * middles + rank - 1)
            return jnp.where(rank == 0, 0, inside)

        below = jnp.where(z > 0, stream_slot(chips - 1 - z) + lag_up, 0)
        above = jnp.where(z < chips - 1, stream_slot(z) + lag_down, 0)
        return jnp.maximum(below, above)

    finish = both_ways(0)
    finish_back = both_ways(1)
    own_count = jnp.where(is_end, pieces, chips)

    total = pieces + HOP_LAG * middles + 2 * CROSS_LAG
    total = max(total, pieces + 2 * items)
    for at in range(1, chips - 1):
        up, down = HOP_LAG * (at - 1), HOP_LAG * (chips - 2 - at)
        longest = max(chips * (chips - 1 - at) + up, chips * at + down)
        total = max(total, pieces + longest + 2 * CROSS_LAG)
        total = max(total, pieces + items + longest)

    def close():
        sent(from_partner, partner_send).wait_send()
        sent(from_partner.at[pl.ds(0, chips - 1)], chain_send).wait_send()

        @pl.when(is_end)
        def _():
            raw_copy(1).wait_send()
            sent(first_in.at[pl.ds(0, pieces)], cross_send.at[middles]).wait_send()
            sent(first_in.at[pl.ds(0, items + pieces)], cross_send.at[middles + 1]).wait_send()

        @pl.when(jnp.logical_not(is_end))
        def _():
            sent(first_in.at[pl.ds(0, chips)], cross_send.at[middles]).wait_send()
            sent(first_in.at[pl.ds(0, items + chips)], cross_send.at[middles + 1]).wait_send()

    item_wait = jnp.where(is_end, END_WAIT, MIDDLE_WAIT)
    work_slots = chips * (chips - 1) // WORK + 1

    def slot_step(slot, carry):
        for k in range(WORK):
            step = chips + WORK * slot + k

            @pl.when(step < chips * chips)
            def _():
                multiply_step(step)
                dest, tile = step_place(step)
                partner_copy(dest, tile, chips - 1 + step // chips).start()

        slab = slot * WORK // chips

        @pl.when(jnp.logical_and(slot * WORK % chips == 0, jnp.logical_and(slab > 0, slab < chips)))
        def _():
            finish_slab(slab)

        @pl.when(slot == work_slots)
        def _():
            split_factor()

        for way in (0, 1):
            index = slot - (lag_down if way else lag_up)
            comes = z < chips - 1 if way else z > 0
            first = 0 if way else chips - 1

            over = index - pieces
            rank = jnp.where(over < 0, 0, 1 + (over // chips) % middles)
            dest = rank if way else chips - 1 - rank
            tile = jnp.where(over < 0, (first + index // 2) % chips, over % chips)
            part = jnp.where(over < 0, index % 2, (over >= items).astype(jnp.int32))
            reaches = dest <= z if way else dest >= z
            sends = dest < z if way else dest > z
            live = jnp.logical_and(index >= 0, over < 2 * items)

            beside = z == (chips - 2 if way else 1)
            opens = jnp.logical_and(index == 0, beside)

            @pl.when(opens)
            def _():
                raw_copy(0).wait_recv()
                raw_copy(1).wait_recv()
                chain_copy(way, dest, tile, part, rest).wait_recv()
                sums[dest, core, tile, part, :raw_rows] = (
                    sums[dest, core, tile, part, :raw_rows] + raw_in[0] + raw_in[1]
                )
                sums[dest, core, tile, part, raw_rows:] = (
                    sums[dest, core, tile, part, raw_rows:]
                    + arrived[dest + 1 - way, tile, part, raw_rows:]
                )

            live = jnp.logical_and(jnp.logical_and(live, comes), reaches)

            @pl.when(jnp.logical_and(live, jnp.logical_not(opens)))
            def _():
                chain_copy(way, dest, tile, part).wait_recv()
                sums[dest, core, tile, part] = (
                    sums[dest, core, tile, part] + arrived[dest + 1 - way, tile, part]
                )

            @pl.when(jnp.logical_and(live, sends))
            def _():
                chain_copy(way, dest, tile, part).start()

        settled = slot - finish_back

        @pl.when(
            jnp.logical_and(jnp.logical_not(is_end), jnp.logical_and(settled >= 0, settled < chips))
        )
        def _():
            columns = pl.ds(pl.multiple_of(settled * wide, wide), wide)
            out_ref[0, half_rows:, columns] = sums[z, core, settled, 1]

        def own_stage(slots_ago, act):
            done = slot - finish - slots_ago

            @pl.when(jnp.logical_and(done >= 0, done < own_count))
            def _():
                tile = jnp.where(is_end, (z + done // 2) % chips, done)
                act(tile, jnp.where(is_end, done % 2, 0), items + done)

        def own_start(tile, part, at):
            first_own(tile, part, at).start()

        def own_mix(tile, part, at):
            first_own(tile, part, at).wait_recv()
            cross_mix(sums[z, core, tile, part], at)

        def own_take(tile, part, at):
            second_copy(at).wait_recv()
            cross_take(mixed[at] + second_in[at], 1 + part, tile)

            @pl.when(at - items >= own_count - jnp.where(is_end, 2, 1))
            def _():
                some = pl.ds(pl.multiple_of(part * half_rows, half_rows), half_rows)

                def store(block, total):
                    out_ref[0, some, block * cb : (block + 1) * cb] = total

                apply_factor(1 + part, store)

        own_stage(0, own_start)

        crossing = slot - item_wait - CROSS_LAG

        @pl.when(jnp.logical_and(crossing >= 0, crossing < items))
        def _():
            dest, tile = item_place(crossing)
            first_item(dest, tile, crossing).wait_recv()
            cross_mix(sums[dest, core, tile, 1], crossing)

        ready = crossing - CROSS_LAG

        @pl.when(jnp.logical_and(ready >= 0, ready < items))
        def _():
            dest, tile = item_place(ready)
            second_copy(ready).wait_recv()
            cross_take(mixed[ready] + second_in[ready], 0, tile)

            @pl.when(tile == chips - 1)
            def _():
                sent(first_in.at[pl.ds(0, chips)], cross_send.at[ready // chips]).wait_send()

                def store(block, total):
                    k = block % per_tile
                    sums[dest, core, block // per_tile, 1, :, k * cb : (k + 1) * cb] = total

                apply_factor(0, store)
                for step in range(chips):
                    end_send(dest, step, 1)

        own_stage(CROSS_LAG, own_mix)
        own_stage(2 * CROSS_LAG, own_take)

        @pl.when(jnp.logical_and(jnp.logical_not(is_end), slot == total - 2))
        def _():
            close()

        return carry

    lax.fori_loop(0, total, slot_step, 0)

    @pl.when(is_end)
    def _():
        close()


def kernel_form(
    pair_devices,
    three_center,
    green_occ,
    green_vir,
    pair_list,
    block_counts,
    cosine_weights,
    coulomb_rows,
    coulomb_blocks,
):
    slots, width, panel = three_center.shape
    chips = pair_devices // 2
    rows = panel // pair_devices
    wide = panel // chips
    piece = (rows // 2, wide)
    blocks, per_block, cb, _ = coulomb_blocks.shape
    normalizer = 1.0 / math.sqrt(slots * width * pair_devices)
    vmem = pl.BlockSpec(memory_space=pltpu.VMEM)
    hbm = pl.BlockSpec(memory_space=pltpu.HBM)
    across = 2 * chips + (chips - 2) * chips
    return pl.pallas_call(
        functools.partial(kernel, chips, normalizer),
        out_shape=pltpu.VMEM((1, rows, panel), jnp.float32),
        in_specs=[hbm] * 8,
        out_specs=vmem,
        scratch_shapes=[
            pltpu.SMEM(pair_list.shape, jnp.int32),
            pltpu.SMEM(block_counts.shape, jnp.int32),
            pltpu.SMEM(cosine_weights.shape, jnp.float32),
            pltpu.SMEM(coulomb_rows.shape[::-1], jnp.int32),
            pltpu.VMEM((chips, slots, width, wide), jnp.bfloat16),
            pltpu.VMEM(green_occ.shape, jnp.bfloat16),
            pltpu.VMEM(green_vir.shape, jnp.bfloat16),
            pltpu.VMEM(coulomb_blocks.shape, jnp.float32),
            pltpu.VMEM((chips, wide, slots * width), jnp.bfloat16),
            pltpu.VMEM((chips, slots * width, wide), jnp.bfloat16),
            pltpu.VMEM((chips, chips, 2) + piece, jnp.float32),
            pltpu.VMEM((chips, 2, chips, 2) + piece, jnp.float32),
            pltpu.VMEM((chips + 1, chips, 2) + piece, jnp.float32),
            pltpu.VMEM((2, rows // 4, wide), jnp.float32),
            pltpu.VMEM((2, rows // 4, wide), jnp.float32),
            pltpu.VMEM((across,) + piece, jnp.float32),
            pltpu.VMEM((across,) + piece, jnp.float32),
            pltpu.VMEM((across,) + piece, jnp.float32),
            pltpu.VMEM((across,) + piece, jnp.float32),
            pltpu.VMEM((3, blocks, rows // 2, cb), jnp.float32),
            pltpu.VMEM((blocks, per_block * cb, cb), jnp.bfloat16),
            pltpu.VMEM((blocks, per_block * cb, cb), jnp.bfloat16),
            pltpu.SemaphoreType.DMA((chips,)),
            pltpu.SemaphoreType.DMA((7,)),
            pltpu.SemaphoreType.DMA,
            pltpu.SemaphoreType.DMA((2 * chips - 1,)),
            pltpu.SemaphoreType.DMA,
            pltpu.SemaphoreType.DMA(((chips + 1) * 2 * chips,)),
            pltpu.SemaphoreType.DMA,
            pltpu.SemaphoreType.DMA((2,)),
            pltpu.SemaphoreType.DMA((chips,)),
            pltpu.SemaphoreType.DMA((2, across)),
        ],
        compiler_params=pltpu.CompilerParams(
            collective_id=0, has_side_effects=True, vmem_limit_bytes=60 * 1024 * 1024
        ),
    )(
        pair_list,
        block_counts,
        cosine_weights,
        coulomb_rows.T,
        three_center,
        green_occ,
        green_vir,
        coulomb_blocks,
    )


def solution(mesh):
    times, pair_devices = mesh.shape["tm"], mesh.shape["pair"]

    def local(*args):
        slots, _, panel = args[0].shape
        cb = args[7].shape[2]
        short = 8 <= pair_devices <= 16 and pair_devices % 2 == 0 and times == 4
        fits = panel % (128 * pair_devices) == 0 and cb % 128 == 0 and slots % 2 == 0
        if short and fits and slots <= 32 and (2 * panel // pair_devices) % cb == 0:
            return kernel_form(pair_devices, *args)
        return collective_form(*args)

    return jax.shard_map(
        local,
        mesh=mesh,
        in_specs=(
            P("pair", None, None),
            P("tm", None, None, None),
            P("tm", None, None, None),
            P("pair"),
            P("pair"),
            P(),
            P(),
            P(),
        ),
        out_specs=P("tm", "pair", None),
        check_vma=False,
    )
```

```python
import functools
import math

import jax
import jax.numpy as jnp
from jax import lax
from jax.experimental import pallas as pl
from jax.experimental.pallas import tpu as pltpu
from jax.sharding import PartitionSpec as P

MESH = pl.DeviceIdType.MESH
HOP_LAG = 3
CROSS_LAG = 3
WORK = 2
END_WAIT = 1
MIDDLE_WAIT = 3


def slab_order(chips):
    order = []
    for z in range(chips):
        if z == 0:
            order.append(list(range(chips - 1, -1, -1)))
        elif z == chips - 1:
            order.append(list(range(chips)))
        else:
            inner = list(range(1, chips - 1))
            if z < chips / 2:
                order.append([chips - 1, 0] + inner[::-1])
            else:
                order.append([0, chips - 1] + inner)
    return order


def half_product(green_matrix, pair_list, alive_mask, three_center):
    slots = pair_list.shape[0]
    picked = jnp.stack(
        [lax.dynamic_index_in_dim(green_matrix[0], pair_list[b], 0, False) for b in range(slots)]
    )
    product = jnp.einsum("bij,bjp->bip", picked, three_center, preferred_element_type=jnp.float32)
    product = product * alive_mask[:, None, None]
    return product.astype(jnp.bfloat16).reshape(-1, three_center.shape[2])


def collective_form(
    three_center,
    green_occ,
    green_vir,
    pair_list,
    block_counts,
    cosine_weights,
    coulomb_rows,
    coulomb_blocks,
):
    slots = three_center.shape[0]
    pair_devices = lax.axis_size("pair")
    alive_mask = (jnp.arange(slots, dtype=jnp.int32) < block_counts[0]).astype(jnp.float32)
    left_side = half_product(green_occ, pair_list, alive_mask, three_center)
    right_side = half_product(green_vir, pair_list, alive_mask, three_center)
    normalizer = 1.0 / math.sqrt(slots * three_center.shape[1] * pair_devices)
    summed = lax.dot_general(
        left_side, right_side, (((0,), (0,)), ((), ())), preferred_element_type=jnp.float32
    )
    row_slab = lax.psum_scatter(summed * normalizer, "pair", scatter_dimension=0, tiled=True)
    transformed = jnp.einsum(
        "ft,trc->frc",
        cosine_weights,
        lax.all_to_all(row_slab[None], "tm", split_axis=2, concat_axis=0, tiled=True),
        precision=lax.Precision.HIGHEST,
    )
    spectra = lax.all_to_all(transformed, "tm", split_axis=0, concat_axis=2, tiled=True)
    rows_here = spectra.shape[1]
    column_blocks = coulomb_rows.shape[0]
    per_column = coulomb_rows.shape[1]
    block_width = coulomb_blocks.shape[2]
    blocked = spectra.reshape(rows_here, column_blocks, block_width)
    picks = coulomb_rows.reshape(-1)
    gathered = jnp.stack(
        [
            lax.dynamic_index_in_dim(blocked, picks[j], 1, False)
            for j in range(column_blocks * per_column)
        ],
        axis=1,
    )
    factors = coulomb_blocks.reshape(column_blocks * per_column, block_width, block_width)
    screened = jnp.einsum("mjx,jxy->mjy", gathered, factors, precision=lax.Precision.HIGHEST)
    screened = screened.reshape(rows_here, column_blocks, per_column, block_width).sum(axis=2)
    return screened.reshape(1, rows_here, column_blocks * block_width)


def kernel(
    chips,
    normalizer,
    pair_list_hbm,
    counts_hbm,
    weights_hbm,
    factor_rows_hbm,
    three_hbm,
    occ_hbm,
    vir_hbm,
    coulomb_hbm,
    out_ref,
    pair_list_ref,
    counts_ref,
    weights_ref,
    factor_rows_ref,
    three,
    occ,
    vir,
    factor,
    left,
    right,
    from_partner,
    sums,
    arrived,
    raw_out,
    raw_in,
    first_in,
    second_out,
    second_in,
    mixed,
    spectra,
    coulomb_high,
    coulomb_low,
    three_sem,
    load_sem,
    partner_send,
    partner_recv,
    chain_send,
    chain_recv,
    raw_send,
    raw_recv,
    cross_send,
    cross_recv,
):
    slots, width = three.shape[1], three.shape[2]
    half_rows, wide = sums.shape[4], sums.shape[5]
    pieces = 2 * chips
    middles = chips - 2
    items = middles * chips
    per_tile = wide // factor.shape[2]
    blocks, per_block, cb = factor.shape[0], factor.shape[1], factor.shape[2]
    me = lax.axis_index("tm")
    place = lax.axis_index("pair")
    z = place // 2
    core = place % 2
    partner = z * 2 + 1 - core
    x_side = me + 1 - 2 * (me % 2)
    y_side = (me + 2) % 4

    def side(stage, at):
        return jnp.where((stage + at) % 2 == 0, x_side, y_side)

    is_end = jnp.logical_or(z == 0, z == chips - 1)

    order = slab_order(chips)

    def slab_at(step):
        dest = 0
        for row in range(chips):
            for k in range(chips):
                hit = jnp.logical_and(z == row, step == k).astype(jnp.int32)
                dest = dest + order[row][k] * hit
        return dest

    head = slab_at(0)

    def three_copy(tile):
        columns = pl.ds(pl.multiple_of(tile * wide, wide), wide)
        return pltpu.make_async_copy(
            three_hbm.at[:, :, columns], three.at[tile], three_sem.at[tile]
        )

    occ_copy = pltpu.make_async_copy(occ_hbm, occ, load_sem.at[0])
    vir_copy = pltpu.make_async_copy(vir_hbm, vir, load_sem.at[1])
    factor_copy = pltpu.make_async_copy(coulomb_hbm, factor, load_sem.at[2])
    list_copy = pltpu.make_async_copy(pair_list_hbm, pair_list_ref, load_sem.at[3])
    counts_copy = pltpu.make_async_copy(counts_hbm, counts_ref, load_sem.at[4])
    weights_copy = pltpu.make_async_copy(weights_hbm, weights_ref, load_sem.at[5])
    rows_copy = pltpu.make_async_copy(factor_rows_hbm, factor_rows_ref, load_sem.at[6])
    occ_copy.start()
    vir_copy.start()
    three_copy(head).start()
    list_copy.start()
    counts_copy.start()

    barrier = pltpu.get_barrier_semaphore()
    pl.semaphore_signal(barrier, inc=1, device_id={"pair": partner}, device_id_type=MESH)
    pl.semaphore_signal(barrier, inc=1, device_id={"tm": x_side}, device_id_type=MESH)
    pl.semaphore_signal(barrier, inc=1, device_id={"tm": y_side}, device_id_type=MESH)

    @pl.when(z > 0)
    def _():
        pl.semaphore_signal(barrier, inc=1, device_id={"pair": place - 2}, device_id_type=MESH)

    @pl.when(z < chips - 1)
    def _():
        pl.semaphore_signal(barrier, inc=1, device_id={"pair": place + 2}, device_id_type=MESH)

    for here, there in ((0, 1), (1, 0), (chips - 1, chips - 2), (chips - 2, chips - 1)):

        @pl.when(z == here)
        def _():
            pl.semaphore_signal(
                barrier, inc=1, device_id={"pair": there * 2 + 1 - core}, device_id_type=MESH
            )

    for step in range(1, chips):
        three_copy((head + step) % chips).start()
    weights_copy.start()
    rows_copy.start()
    factor_copy.start()

    list_copy.wait()
    counts_copy.wait()
    occ_copy.wait()
    vir_copy.wait()
    neighbours = (z > 0).astype(jnp.int32) + (z < chips - 1).astype(jnp.int32)
    for here in (0, 1, chips - 2, chips - 1):
        neighbours = neighbours + (z == here).astype(jnp.int32)

    def half_tile(tile):
        three_copy(tile).wait()
        for first in range(0, slots, 2):
            lefts = []
            for slot in (first, first + 1):
                group = pair_list_ref[slot]
                alive = (slot < counts_ref[0]).astype(jnp.bfloat16)
                both = jnp.concatenate([occ[0, group], vir[0, group]], axis=0) * alive
                product = jnp.dot(both, three[tile, slot], preferred_element_type=jnp.float32)
                product = product.astype(jnp.bfloat16)
                lefts.append(product[:width])
                right[tile, slot * width : (slot + 1) * width, :] = product[width:]
            left[tile, :, first * width : (first + 2) * width] = jnp.concatenate(lefts, axis=0).T

    def partner_copy(dest, tile, at):
        return pltpu.make_async_remote_copy(
            src_ref=sums.at[dest, 1 - core, tile],
            dst_ref=from_partner.at[dest, tile],
            send_sem=partner_send,
            recv_sem=partner_recv.at[at],
            device_id={"pair": partner},
            device_id_type=MESH,
        )

    def sent(bytes_of, send_sem):
        return pltpu.make_async_remote_copy(
            src_ref=bytes_of,
            dst_ref=bytes_of,
            send_sem=send_sem,
            recv_sem=partner_recv.at[0],
            device_id={"pair": partner},
            device_id_type=MESH,
        )

    def chain_copy(way, dest, tile, part, rows=slice(None)):
        place_at = dest + 1 - way
        rows = pl.ds(rows.start or 0, half_rows - (rows.start or 0))
        return pltpu.make_async_remote_copy(
            src_ref=sums.at[dest, core, tile, part, rows],
            dst_ref=arrived.at[place_at, tile, part, rows],
            send_sem=chain_send,
            recv_sem=chain_recv.at[place_at * pieces + part * chips + tile],
            device_id={"pair": place + 2 - 4 * way},
            device_id_type=MESH,
        )

    raw_rows = raw_in.shape[1]
    rest = slice(raw_rows, None)

    def raw_copy(across):
        there = jnp.where(z == 0, 1, chips - 2) * 2 + (1 - core if across else core)
        return pltpu.make_async_remote_copy(
            src_ref=raw_out.at[across],
            dst_ref=raw_in.at[across],
            send_sem=raw_send if across else chain_send,
            recv_sem=raw_recv.at[across],
            device_id={"pair": there},
            device_id_type=MESH,
        )

    def cross_copy(source, target, stage, send_at, recv_at):
        return pltpu.make_async_remote_copy(
            src_ref=source,
            dst_ref=target,
            send_sem=cross_send.at[send_at],
            recv_sem=cross_recv.at[stage, recv_at],
            device_id={"tm": side(stage, recv_at)},
            device_id_type=MESH,
        )

    def first_item(dest, tile, item):
        source = sums.at[dest, core, tile, 1]
        return cross_copy(source, first_in.at[item], 0, item // chips, item)

    def second_copy(at):
        return cross_copy(second_out.at[at], second_in.at[at], 1, middles + 1, at)

    def first_own(tile, part, at):
        return cross_copy(sums.at[z, core, tile, part], first_in.at[at], 0, middles, at)

    def end_send(dest, tile, part, rows=slice(None)):
        @pl.when(jnp.logical_and(z == 0, dest > z))
        def _():
            chain_copy(0, dest, tile, part, rows).start()

        @pl.when(jnp.logical_and(z == chips - 1, dest < z))
        def _():
            chain_copy(1, dest, tile, part, rows).start()

    def step_place(step):
        dest = slab_at(step // chips)
        return dest, jnp.where(step < chips, (head + step) % chips, step % chips)

    early = z < (chips + 1) // 2

    def item_place(item):
        rank = item // chips
        return jnp.where(early, chips - 2 - rank, 1 + rank), item % chips

    def item_at(dest, tile):
        return jnp.where(early, chips - 2 - dest, dest - 1) * chips + tile

    def head_tile(step):
        return (head + step) % chips

    def finish_head(step):
        tile = head_tile(step)
        partner_copy(head, tile, step).wait_recv()
        sums[head, core, tile] = sums[head, core, tile] + from_partner[head, tile]

        @pl.when(step == 0)
        def _():
            end_send(head, tile, 0, rest)

        @pl.when(step > 0)
        def _():
            end_send(head, tile, 0)

        end_send(head, tile, 1)

    def finish_slab(at):
        dest = slab_at(at)
        inner = jnp.logical_and(dest > 0, dest < chips - 1)
        pltpu.make_async_remote_copy(
            src_ref=sums.at[dest, 1 - core],
            dst_ref=from_partner.at[dest],
            send_sem=partner_send,
            recv_sem=partner_recv.at[chips - 1 + at],
            device_id={"pair": partner},
            device_id_type=MESH,
        ).wait_recv()

        def tile_step(tile, carry):
            sums[dest, core, tile] = sums[dest, core, tile] + from_partner[dest, tile]

            @pl.when(inner)
            def _():
                end_send(dest, tile, 0)
                first_item(dest, tile, item_at(dest, tile)).start()

            return carry

        lax.fori_loop(0, chips, tile_step, 0)

    def multiply_step(step):
        dest, tile = step_place(step)
        product = jnp.dot(left[dest], right[tile], preferred_element_type=jnp.float32)
        product = product.reshape(2, 2, half_rows, wide)
        sums[dest, 0, tile] = product[0]
        sums[dest, 1, tile] = product[1]

    def head_step(step, carry):
        half_tile(head_tile(step))
        multiply_step(step)

        @pl.when(step == 0)
        def _():
            pl.semaphore_wait(barrier, 3 + neighbours)

        partner_copy(head, head_tile(step), step).start()

        @pl.when(jnp.logical_and(is_end, step == 0))
        def _():
            raw_out[0] = sums[head, core, head, 0, :raw_rows]
            raw_out[1] = sums[head, 1 - core, head, 0, :raw_rows]
            raw_copy(0).start()
            raw_copy(1).start()

        @pl.when(step > 0)
        def _():
            finish_head(step - 1)

        return carry

    lax.fori_loop(0, chips, head_step, 0)
    finish_head(chips - 1)
    weights_copy.wait()
    rows_copy.wait()

    def split_factor():
        factor_copy.wait()
        for block in range(blocks):
            exact = factor[block].reshape(per_block * cb, cb)
            high = exact.astype(jnp.bfloat16)
            coulomb_high[block] = high
            coulomb_low[block] = (exact - high.astype(jnp.float32)).astype(jnp.bfloat16)

    def apply_factor(held, store):
        for block in range(blocks):
            gathered = jnp.concatenate(
                [spectra[held, factor_rows_ref[k, block]] for k in range(per_block)], axis=1
            )
            high = gathered.astype(jnp.bfloat16)
            low = (gathered - high.astype(jnp.float32)).astype(jnp.bfloat16)
            total = jnp.dot(high, coulomb_high[block], preferred_element_type=jnp.float32)
            total += jnp.dot(low, coulomb_high[block], preferred_element_type=jnp.float32)
            total += jnp.dot(high, coulomb_low[block], preferred_element_type=jnp.float32)
            store(block, total)

    def weight(f, t):
        return weights_ref[f, t] * normalizer

    def cross_mix(own, at):
        other = first_in[at]
        near, far = side(0, at), side(1, at)
        second_out[at] = own * weight(far, me) + other * weight(far, near)
        mixed[at] = own * weight(me, me) + other * weight(me, near)
        second_copy(at).start()

    def cross_take(whole, held, tile):
        for k in range(per_tile):
            spectra[held, tile * per_tile + k] = whole[:, k * cb : (k + 1) * cb]

    lag_up = HOP_LAG * jnp.maximum(z - 1, 0)
    lag_down = HOP_LAG * jnp.maximum(chips - 2 - z, 0)

    def both_ways(part):
        def stream_slot(rank):
            inside = pieces + chips * (part * middles + rank - 1)
            return jnp.where(rank == 0, 0, inside)

        below = jnp.where(z > 0, stream_slot(chips - 1 - z) + lag_up, 0)
        above = jnp.where(z < chips - 1, stream_slot(z) + lag_down, 0)
        return jnp.maximum(below, above)

    finish = both_ways(0)
    finish_back = both_ways(1)
    own_count = jnp.where(is_end, pieces, chips)

    total = pieces + HOP_LAG * middles + 2 * CROSS_LAG
    total = max(total, pieces + 2 * items)
    for at in range(1, chips - 1):
        up, down = HOP_LAG * (at - 1), HOP_LAG * (chips - 2 - at)
        longest = max(chips * (chips - 1 - at) + up, chips * at + down)
        total = max(total, pieces + longest + 2 * CROSS_LAG)
        total = max(total, pieces + items + longest)

    def close():
        sent(from_partner, partner_send).wait_send()
        sent(from_partner.at[pl.ds(0, chips - 1)], chain_send).wait_send()

        @pl.when(is_end)
        def _():
            raw_copy(1).wait_send()
            sent(first_in.at[pl.ds(0, pieces)], cross_send.at[middles]).wait_send()
            sent(first_in.at[pl.ds(0, items + pieces)], cross_send.at[middles + 1]).wait_send()

        @pl.when(jnp.logical_not(is_end))
        def _():
            sent(first_in.at[pl.ds(0, chips)], cross_send.at[middles]).wait_send()
            sent(first_in.at[pl.ds(0, items + chips)], cross_send.at[middles + 1]).wait_send()

    item_wait = jnp.where(is_end, END_WAIT, MIDDLE_WAIT)
    work_slots = chips * (chips - 1) // WORK + 1

    def slot_step(slot, carry):
        for k in range(WORK):
            step = chips + WORK * slot + k

            @pl.when(step < chips * chips)
            def _():
                multiply_step(step)
                dest, tile = step_place(step)
                partner_copy(dest, tile, chips - 1 + step // chips).start()

        slab = slot * WORK // chips

        @pl.when(jnp.logical_and(slot * WORK % chips == 0, jnp.logical_and(slab > 0, slab < chips)))
        def _():
            finish_slab(slab)

        @pl.when(slot == work_slots)
        def _():
            split_factor()

        for way in (0, 1):
            index = slot - (lag_down if way else lag_up)
            comes = z < chips - 1 if way else z > 0
            first = 0 if way else chips - 1

            over = index - pieces
            rank = jnp.where(over < 0, 0, 1 + (over // chips) % middles)
            dest = rank if way else chips - 1 - rank
            tile = jnp.where(over < 0, (first + index // 2) % chips, over % chips)
            part = jnp.where(over < 0, index % 2, (over >= items).astype(jnp.int32))
            reaches = dest <= z if way else dest >= z
            sends = dest < z if way else dest > z
            live = jnp.logical_and(index >= 0, over < 2 * items)

            beside = z == (chips - 2 if way else 1)
            opens = jnp.logical_and(index == 0, beside)

            @pl.when(opens)
            def _():
                raw_copy(0).wait_recv()
                raw_copy(1).wait_recv()
                chain_copy(way, dest, tile, part, rest).wait_recv()
                sums[dest, core, tile, part, :raw_rows] = (
                    sums[dest, core, tile, part, :raw_rows] + raw_in[0] + raw_in[1]
                )
                sums[dest, core, tile, part, raw_rows:] = (
                    sums[dest, core, tile, part, raw_rows:]
                    + arrived[dest + 1 - way, tile, part, raw_rows:]
                )

            live = jnp.logical_and(jnp.logical_and(live, comes), reaches)

            @pl.when(jnp.logical_and(live, jnp.logical_not(opens)))
            def _():
                chain_copy(way, dest, tile, part).wait_recv()
                sums[dest, core, tile, part] = (
                    sums[dest, core, tile, part] + arrived[dest + 1 - way, tile, part]
                )

            @pl.when(jnp.logical_and(live, sends))
            def _():
                chain_copy(way, dest, tile, part).start()

        settled = slot - finish_back

        @pl.when(
            jnp.logical_and(jnp.logical_not(is_end), jnp.logical_and(settled >= 0, settled < chips))
        )
        def _():
            columns = pl.ds(pl.multiple_of(settled * wide, wide), wide)
            out_ref[0, half_rows:, columns] = sums[z, core, settled, 1]

        def own_stage(slots_ago, act):
            done = slot - finish - slots_ago

            @pl.when(jnp.logical_and(done >= 0, done < own_count))
            def _():
                tile = jnp.where(is_end, (z + done // 2) % chips, done)
                act(tile, jnp.where(is_end, done % 2, 0), items + done)

        def own_start(tile, part, at):
            first_own(tile, part, at).start()

        def own_mix(tile, part, at):
            first_own(tile, part, at).wait_recv()
            cross_mix(sums[z, core, tile, part], at)

        def own_take(tile, part, at):
            second_copy(at).wait_recv()
            cross_take(mixed[at] + second_in[at], 1 + part, tile)

            @pl.when(at - items >= own_count - jnp.where(is_end, 2, 1))
            def _():
                some = pl.ds(pl.multiple_of(part * half_rows, half_rows), half_rows)

                def store(block, total):
                    out_ref[0, some, block * cb : (block + 1) * cb] = total

                apply_factor(1 + part, store)

        own_stage(0, own_start)

        crossing = slot - item_wait - CROSS_LAG

        @pl.when(jnp.logical_and(crossing >= 0, crossing < items))
        def _():
            dest, tile = item_place(crossing)
            first_item(dest, tile, crossing).wait_recv()
            cross_mix(sums[dest, core, tile, 1], crossing)

        ready = crossing - CROSS_LAG

        @pl.when(jnp.logical_and(ready >= 0, ready < items))
        def _():
            dest, tile = item_place(ready)
            second_copy(ready).wait_recv()
            cross_take(mixed[ready] + second_in[ready], 0, tile)

            @pl.when(tile == chips - 1)
            def _():
                sent(first_in.at[pl.ds(0, chips)], cross_send.at[ready // chips]).wait_send()

                def store(block, total):
                    k = block % per_tile
                    sums[dest, core, block // per_tile, 1, :, k * cb : (k + 1) * cb] = total

                apply_factor(0, store)
                for step in range(chips):
                    end_send(dest, step, 1)

        own_stage(CROSS_LAG, own_mix)
        own_stage(2 * CROSS_LAG, own_take)

        @pl.when(jnp.logical_and(jnp.logical_not(is_end), slot == total - 2))
        def _():
            close()

        return carry

    lax.fori_loop(0, total, slot_step, 0)

    @pl.when(is_end)
    def _():
        close()


def kernel_form(
    pair_devices,
    three_center,
    green_occ,
    green_vir,
    pair_list,
    block_counts,
    cosine_weights,
    coulomb_rows,
    coulomb_blocks,
):
    slots, width, panel = three_center.shape
    chips = pair_devices // 2
    rows = panel // pair_devices
    wide = panel // chips
    piece = (rows // 2, wide)
    blocks, per_block, cb, _ = coulomb_blocks.shape
    normalizer = 1.0 / math.sqrt(slots * width * pair_devices)
    vmem = pl.BlockSpec(memory_space=pltpu.VMEM)
    hbm = pl.BlockSpec(memory_space=pltpu.HBM)
    across = 2 * chips + (chips - 2) * chips
    return pl.pallas_call(
        functools.partial(kernel, chips, normalizer),
        out_shape=pltpu.VMEM((1, rows, panel), jnp.float32),
        in_specs=[hbm] * 8,
        out_specs=vmem,
        scratch_shapes=[
            pltpu.SMEM(pair_list.shape, jnp.int32),
            pltpu.SMEM(block_counts.shape, jnp.int32),
            pltpu.SMEM(cosine_weights.shape, jnp.float32),
            pltpu.SMEM(coulomb_rows.shape[::-1], jnp.int32),
            pltpu.VMEM((chips, slots, width, wide), jnp.bfloat16),
            pltpu.VMEM(green_occ.shape, jnp.bfloat16),
            pltpu.VMEM(green_vir.shape, jnp.bfloat16),
            pltpu.VMEM(coulomb_blocks.shape, jnp.float32),
            pltpu.VMEM((chips, wide, slots * width), jnp.bfloat16),
            pltpu.VMEM((chips, slots * width, wide), jnp.bfloat16),
            pltpu.VMEM((chips, chips, 2) + piece, jnp.float32),
            pltpu.VMEM((chips, 2, chips, 2) + piece, jnp.float32),
            pltpu.VMEM((chips + 1, chips, 2) + piece, jnp.float32),
            pltpu.VMEM((2, rows // 4, wide), jnp.float32),
            pltpu.VMEM((2, rows // 4, wide), jnp.float32),
            pltpu.VMEM((across,) + piece, jnp.float32),
            pltpu.VMEM((across,) + piece, jnp.float32),
            pltpu.VMEM((across,) + piece, jnp.float32),
            pltpu.VMEM((across,) + piece, jnp.float32),
            pltpu.VMEM((3, blocks, rows // 2, cb), jnp.float32),
            pltpu.VMEM((blocks, per_block * cb, cb), jnp.bfloat16),
            pltpu.VMEM((blocks, per_block * cb, cb), jnp.bfloat16),
            pltpu.SemaphoreType.DMA((chips,)),
            pltpu.SemaphoreType.DMA((7,)),
            pltpu.SemaphoreType.DMA,
            pltpu.SemaphoreType.DMA((2 * chips - 1,)),
            pltpu.SemaphoreType.DMA,
            pltpu.SemaphoreType.DMA(((chips + 1) * 2 * chips,)),
            pltpu.SemaphoreType.DMA,
            pltpu.SemaphoreType.DMA((2,)),
            pltpu.SemaphoreType.DMA((chips,)),
            pltpu.SemaphoreType.DMA((2, across)),
        ],
        compiler_params=pltpu.CompilerParams(
            collective_id=0, has_side_effects=True, vmem_limit_bytes=60 * 1024 * 1024
        ),
    )(
        pair_list,
        block_counts,
        cosine_weights,
        coulomb_rows.T,
        three_center,
        green_occ,
        green_vir,
        coulomb_blocks,
    )


def solution(mesh):
    times, pair_devices = mesh.shape["tm"], mesh.shape["pair"]

    def local(*args):
        slots, _, panel = args[0].shape
        cb = args[7].shape[2]
        short = 8 <= pair_devices <= 16 and pair_devices % 2 == 0 and times == 4
        fits = panel % (128 * pair_devices) == 0 and cb % 128 == 0 and slots % 2 == 0
        if short and fits and slots <= 32 and (2 * panel // pair_devices) % cb == 0:
            return kernel_form(pair_devices, *args)
        return collective_form(*args)

    return jax.shard_map(
        local,
        mesh=mesh,
        in_specs=(
            P("pair", None, None),
            P("tm", None, None, None),
            P("tm", None, None, None),
            P("pair"),
            P("pair"),
            P(),
            P(),
            P(),
        ),
        out_specs=P("tm", "pair", None),
        check_vma=False,
    )
```

```python
import functools
import math

import jax
import jax.numpy as jnp
from jax import lax
from jax.experimental import pallas as pl
from jax.experimental.pallas import tpu as pltpu
from jax.sharding import PartitionSpec as P

MESH = pl.DeviceIdType.MESH
HOP_LAG = 3
CROSS_LAG = 3
WORK = 2
END_WAIT = 1
MIDDLE_WAIT = 3


def slab_order(chips):
    order = []
    for z in range(chips):
        if z == 0:
            order.append(list(range(chips - 1, -1, -1)))
        elif z == chips - 1:
            order.append(list(range(chips)))
        else:
            inner = list(range(1, chips - 1))
            if z < chips / 2:
                order.append([chips - 1, 0] + inner[::-1])
            else:
                order.append([0, chips - 1] + inner)
    return order


def half_product(green_matrix, pair_list, alive_mask, three_center):
    slots = pair_list.shape[0]
    picked = jnp.stack(
        [lax.dynamic_index_in_dim(green_matrix[0], pair_list[b], 0, False) for b in range(slots)]
    )
    product = jnp.einsum("bij,bjp->bip", picked, three_center, preferred_element_type=jnp.float32)
    product = product * alive_mask[:, None, None]
    return product.astype(jnp.bfloat16).reshape(-1, three_center.shape[2])


def collective_form(
    three_center,
    green_occ,
    green_vir,
    pair_list,
    block_counts,
    cosine_weights,
    coulomb_rows,
    coulomb_blocks,
):
    slots = three_center.shape[0]
    pair_devices = lax.axis_size("pair")
    alive_mask = (jnp.arange(slots, dtype=jnp.int32) < block_counts[0]).astype(jnp.float32)
    left_side = half_product(green_occ, pair_list, alive_mask, three_center)
    right_side = half_product(green_vir, pair_list, alive_mask, three_center)
    normalizer = 1.0 / math.sqrt(slots * three_center.shape[1] * pair_devices)
    summed = lax.dot_general(
        left_side, right_side, (((0,), (0,)), ((), ())), preferred_element_type=jnp.float32
    )
    row_slab = lax.psum_scatter(summed * normalizer, "pair", scatter_dimension=0, tiled=True)
    transformed = jnp.einsum(
        "ft,trc->frc",
        cosine_weights,
        lax.all_to_all(row_slab[None], "tm", split_axis=2, concat_axis=0, tiled=True),
        precision=lax.Precision.HIGHEST,
    )
    spectra = lax.all_to_all(transformed, "tm", split_axis=0, concat_axis=2, tiled=True)
    rows_here = spectra.shape[1]
    column_blocks = coulomb_rows.shape[0]
    per_column = coulomb_rows.shape[1]
    block_width = coulomb_blocks.shape[2]
    blocked = spectra.reshape(rows_here, column_blocks, block_width)
    picks = coulomb_rows.reshape(-1)
    gathered = jnp.stack(
        [
            lax.dynamic_index_in_dim(blocked, picks[j], 1, False)
            for j in range(column_blocks * per_column)
        ],
        axis=1,
    )
    factors = coulomb_blocks.reshape(column_blocks * per_column, block_width, block_width)
    screened = jnp.einsum("mjx,jxy->mjy", gathered, factors, precision=lax.Precision.HIGHEST)
    screened = screened.reshape(rows_here, column_blocks, per_column, block_width).sum(axis=2)
    return screened.reshape(1, rows_here, column_blocks * block_width)


def kernel(
    chips,
    normalizer,
    pair_list_hbm,
    counts_hbm,
    weights_hbm,
    factor_rows_hbm,
    three_hbm,
    occ_hbm,
    vir_hbm,
    coulomb_hbm,
    out_ref,
    pair_list_ref,
    counts_ref,
    weights_ref,
    factor_rows_ref,
    three,
    occ,
    vir,
    factor,
    left,
    right,
    from_partner,
    sums,
    arrived,
    raw_out,
    raw_in,
    first_in,
    second_out,
    second_in,
    mixed,
    spectra,
    coulomb_high,
    coulomb_low,
    three_sem,
    load_sem,
    partner_send,
    partner_recv,
    chain_send,
    chain_recv,
    raw_send,
    raw_recv,
    cross_send,
    cross_recv,
):
    slots, width = three.shape[1], three.shape[2]
    half_rows, wide = sums.shape[4], sums.shape[5]
    pieces = 2 * chips
    middles = chips - 2
    items = middles * chips
    per_tile = wide // factor.shape[2]
    blocks, per_block, cb = factor.shape[0], factor.shape[1], factor.shape[2]
    me = lax.axis_index("tm")
    place = lax.axis_index("pair")
    z = place // 2
    core = place % 2
    partner = z * 2 + 1 - core
    x_side = me + 1 - 2 * (me % 2)
    y_side = (me + 2) % 4

    def side(stage, at):
        return jnp.where((stage + at) % 2 == 0, x_side, y_side)

    is_end = jnp.logical_or(z == 0, z == chips - 1)

    order = slab_order(chips)

    def slab_at(step):
        dest = 0
        for row in range(chips):
            for k in range(chips):
                hit = jnp.logical_and(z == row, step == k).astype(jnp.int32)
                dest = dest + order[row][k] * hit
        return dest

    head = slab_at(0)

    def three_copy(tile):
        columns = pl.ds(pl.multiple_of(tile * wide, wide), wide)
        return pltpu.make_async_copy(
            three_hbm.at[:, :, columns], three.at[tile], three_sem.at[tile]
        )

    occ_copy = pltpu.make_async_copy(occ_hbm, occ, load_sem.at[0])
    vir_copy = pltpu.make_async_copy(vir_hbm, vir, load_sem.at[1])
    factor_copy = pltpu.make_async_copy(coulomb_hbm, factor, load_sem.at[2])
    list_copy = pltpu.make_async_copy(pair_list_hbm, pair_list_ref, load_sem.at[3])
    counts_copy = pltpu.make_async_copy(counts_hbm, counts_ref, load_sem.at[4])
    weights_copy = pltpu.make_async_copy(weights_hbm, weights_ref, load_sem.at[5])
    rows_copy = pltpu.make_async_copy(factor_rows_hbm, factor_rows_ref, load_sem.at[6])
    occ_copy.start()
    vir_copy.start()
    three_copy(head).start()
    list_copy.start()
    counts_copy.start()

    barrier = pltpu.get_barrier_semaphore()
    pl.semaphore_signal(barrier, inc=1, device_id={"pair": partner}, device_id_type=MESH)
    pl.semaphore_signal(barrier, inc=1, device_id={"tm": x_side}, device_id_type=MESH)
    pl.semaphore_signal(barrier, inc=1, device_id={"tm": y_side}, device_id_type=MESH)

    @pl.when(z > 0)
    def _():
        pl.semaphore_signal(barrier, inc=1, device_id={"pair": place - 2}, device_id_type=MESH)

    @pl.when(z < chips - 1)
    def _():
        pl.semaphore_signal(barrier, inc=1, device_id={"pair": place + 2}, device_id_type=MESH)

    for here, there in ((0, 1), (1, 0), (chips - 1, chips - 2), (chips - 2, chips - 1)):

        @pl.when(z == here)
        def _():
            pl.semaphore_signal(
                barrier, inc=1, device_id={"pair": there * 2 + 1 - core}, device_id_type=MESH
            )

    for step in range(1, chips):
        three_copy((head + step) % chips).start()
    weights_copy.start()
    rows_copy.start()
    factor_copy.start()

    list_copy.wait()
    counts_copy.wait()
    occ_copy.wait()
    vir_copy.wait()
    neighbours = (z > 0).astype(jnp.int32) + (z < chips - 1).astype(jnp.int32)
    for here in (0, 1, chips - 2, chips - 1):
        neighbours = neighbours + (z == here).astype(jnp.int32)

    def half_tile(tile):
        three_copy(tile).wait()
        for first in range(0, slots, 2):
            lefts = []
            for slot in (first, first + 1):
                group = pair_list_ref[slot]
                alive = (slot < counts_ref[0]).astype(jnp.bfloat16)
                both = jnp.concatenate([occ[0, group], vir[0, group]], axis=0) * alive
                product = jnp.dot(both, three[tile, slot], preferred_element_type=jnp.float32)
                product = product.astype(jnp.bfloat16)
                lefts.append(product[:width])
                right[tile, slot * width : (slot + 1) * width, :] = product[width:]
            left[tile, :, first * width : (first + 2) * width] = jnp.concatenate(lefts, axis=0).T

    def partner_copy(dest, tile, at):
        return pltpu.make_async_remote_copy(
            src_ref=sums.at[dest, 1 - core, tile],
            dst_ref=from_partner.at[dest, tile],
            send_sem=partner_send,
            recv_sem=partner_recv.at[at],
            device_id={"pair": partner},
            device_id_type=MESH,
        )

    def sent(bytes_of, send_sem):
        return pltpu.make_async_remote_copy(
            src_ref=bytes_of,
            dst_ref=bytes_of,
            send_sem=send_sem,
            recv_sem=partner_recv.at[0],
            device_id={"pair": partner},
            device_id_type=MESH,
        )

    def chain_copy(way, dest, tile, part, rows=slice(None)):
        place_at = dest + 1 - way
        rows = pl.ds(rows.start or 0, half_rows - (rows.start or 0))
        return pltpu.make_async_remote_copy(
            src_ref=sums.at[dest, core, tile, part, rows],
            dst_ref=arrived.at[place_at, tile, part, rows],
            send_sem=chain_send,
            recv_sem=chain_recv.at[place_at * pieces + part * chips + tile],
            device_id={"pair": place + 2 - 4 * way},
            device_id_type=MESH,
        )

    raw_rows = raw_in.shape[1]
    rest = slice(raw_rows, None)

    def raw_copy(across):
        there = jnp.where(z == 0, 1, chips - 2) * 2 + (1 - core if across else core)
        return pltpu.make_async_remote_copy(
            src_ref=raw_out.at[across],
            dst_ref=raw_in.at[across],
            send_sem=raw_send if across else chain_send,
            recv_sem=raw_recv.at[across],
            device_id={"pair": there},
            device_id_type=MESH,
        )

    def cross_copy(source, target, stage, send_at, recv_at):
        return pltpu.make_async_remote_copy(
            src_ref=source,
            dst_ref=target,
            send_sem=cross_send.at[send_at],
            recv_sem=cross_recv.at[stage, recv_at],
            device_id={"tm": side(stage, recv_at)},
            device_id_type=MESH,
        )

    def first_item(dest, tile, item):
        source = sums.at[dest, core, tile, 1]
        return cross_copy(source, first_in.at[item], 0, item // chips, item)

    def second_copy(at):
        return cross_copy(second_out.at[at], second_in.at[at], 1, middles + 1, at)

    def first_own(tile, part, at):
        return cross_copy(sums.at[z, core, tile, part], first_in.at[at], 0, middles, at)

    def end_send(dest, tile, part, rows=slice(None)):
        @pl.when(jnp.logical_and(z == 0, dest > z))
        def _():
            chain_copy(0, dest, tile, part, rows).start()

        @pl.when(jnp.logical_and(z == chips - 1, dest < z))
        def _():
            chain_copy(1, dest, tile, part, rows).start()

    def step_place(step):
        dest = slab_at(step // chips)
        return dest, jnp.where(step < chips, (head + step) % chips, step % chips)

    early = z < (chips + 1) // 2

    def item_place(item):
        rank = item // chips
        return jnp.where(early, chips - 2 - rank, 1 + rank), item % chips

    def item_at(dest, tile):
        return jnp.where(early, chips - 2 - dest, dest - 1) * chips + tile

    def head_tile(step):
        return (head + step) % chips

    def finish_head(step):
        tile = head_tile(step)
        partner_copy(head, tile, step).wait_recv()
        sums[head, core, tile] = sums[head, core, tile] + from_partner[head, tile]

        @pl.when(step == 0)
        def _():
            end_send(head, tile, 0, rest)

        @pl.when(step > 0)
        def _():
            end_send(head, tile, 0)

        end_send(head, tile, 1)

    def finish_slab(at):
        dest = slab_at(at)
        inner = jnp.logical_and(dest > 0, dest < chips - 1)
        pltpu.make_async_remote_copy(
            src_ref=sums.at[dest, 1 - core],
            dst_ref=from_partner.at[dest],
            send_sem=partner_send,
            recv_sem=partner_recv.at[chips - 1 + at],
            device_id={"pair": partner},
            device_id_type=MESH,
        ).wait_recv()

        def tile_step(tile, carry):
            sums[dest, core, tile] = sums[dest, core, tile] + from_partner[dest, tile]

            @pl.when(inner)
            def _():
                end_send(dest, tile, 0)
                first_item(dest, tile, item_at(dest, tile)).start()

            return carry

        lax.fori_loop(0, chips, tile_step, 0)

    def multiply_step(step):
        dest, tile = step_place(step)
        product = jnp.dot(left[dest], right[tile], preferred_element_type=jnp.float32)
        product = product.reshape(2, 2, half_rows, wide)
        sums[dest, 0, tile] = product[0]
        sums[dest, 1, tile] = product[1]

    def head_step(step, carry):
        half_tile(head_tile(step))
        multiply_step(step)

        @pl.when(step == 0)
        def _():
            pl.semaphore_wait(barrier, 3 + neighbours)

        partner_copy(head, head_tile(step), step).start()

        @pl.when(jnp.logical_and(is_end, step == 0))
        def _():
            raw_out[0] = sums[head, core, head, 0, :raw_rows]
            raw_out[1] = sums[head, 1 - core, head, 0, :raw_rows]
            raw_copy(0).start()
            raw_copy(1).start()

        @pl.when(step > 0)
        def _():
            finish_head(step - 1)

        return carry

    lax.fori_loop(0, chips, head_step, 0)
    finish_head(chips - 1)
    weights_copy.wait()
    rows_copy.wait()

    def split_factor():
        factor_copy.wait()
        for block in range(blocks):
            exact = factor[block].reshape(per_block * cb, cb)
            high = exact.astype(jnp.bfloat16)
            coulomb_high[block] = high
            coulomb_low[block] = (exact - high.astype(jnp.float32)).astype(jnp.bfloat16)

    def apply_factor(held, store):
        for block in range(blocks):
            gathered = jnp.concatenate(
                [spectra[held, factor_rows_ref[k, block]] for k in range(per_block)], axis=1
            )
            high = gathered.astype(jnp.bfloat16)
            low = (gathered - high.astype(jnp.float32)).astype(jnp.bfloat16)
            total = jnp.dot(high, coulomb_high[block], preferred_element_type=jnp.float32)
            total += jnp.dot(low, coulomb_high[block], preferred_element_type=jnp.float32)
            total += jnp.dot(high, coulomb_low[block], preferred_element_type=jnp.float32)
            store(block, total)

    def weight(f, t):
        return weights_ref[f, t] * normalizer

    def cross_mix(own, at):
        other = first_in[at]
        near, far = side(0, at), side(1, at)
        second_out[at] = own * weight(far, me) + other * weight(far, near)
        mixed[at] = own * weight(me, me) + other * weight(me, near)
        second_copy(at).start()

    def cross_take(whole, held, tile):
        for k in range(per_tile):
            spectra[held, tile * per_tile + k] = whole[:, k * cb : (k + 1) * cb]

    lag_up = HOP_LAG * jnp.maximum(z - 1, 0)
    lag_down = HOP_LAG * jnp.maximum(chips - 2 - z, 0)

    def both_ways(part):
        def stream_slot(rank):
            inside = pieces + chips * (part * middles + rank - 1)
            return jnp.where(rank == 0, 0, inside)

        below = jnp.where(z > 0, stream_slot(chips - 1 - z) + lag_up, 0)
        above = jnp.where(z < chips - 1, stream_slot(z) + lag_down, 0)
        return jnp.maximum(below, above)

    finish = both_ways(0)
    finish_back = both_ways(1)
    own_count = jnp.where(is_end, pieces, chips)

    total = pieces + HOP_LAG * middles + 2 * CROSS_LAG
    total = max(total, pieces + 2 * items)
    for at in range(1, chips - 1):
        up, down = HOP_LAG * (at - 1), HOP_LAG * (chips - 2 - at)
        longest = max(chips * (chips - 1 - at) + up, chips * at + down)
        total = max(total, pieces + longest + 2 * CROSS_LAG)
        total = max(total, pieces + items + longest)

    def close():
        sent(from_partner, partner_send).wait_send()
        sent(from_partner.at[pl.ds(0, chips - 1)], chain_send).wait_send()

        @pl.when(is_end)
        def _():
            raw_copy(1).wait_send()
            sent(first_in.at[pl.ds(0, pieces)], cross_send.at[middles]).wait_send()
            sent(first_in.at[pl.ds(0, items + pieces)], cross_send.at[middles + 1]).wait_send()

        @pl.when(jnp.logical_not(is_end))
        def _():
            sent(first_in.at[pl.ds(0, chips)], cross_send.at[middles]).wait_send()
            sent(first_in.at[pl.ds(0, items + chips)], cross_send.at[middles + 1]).wait_send()

    item_wait = jnp.where(is_end, END_WAIT, MIDDLE_WAIT)
    work_slots = chips * (chips - 1) // WORK + 1

    def slot_step(slot, carry):
        for k in range(WORK):
            step = chips + WORK * slot + k

            @pl.when(step < chips * chips)
            def _():
                multiply_step(step)
                dest, tile = step_place(step)
                partner_copy(dest, tile, chips - 1 + step // chips).start()

        slab = slot * WORK // chips

        @pl.when(jnp.logical_and(slot * WORK % chips == 0, jnp.logical_and(slab > 0, slab < chips)))
        def _():
            finish_slab(slab)

        @pl.when(slot == work_slots)
        def _():
            split_factor()

        for way in (0, 1):
            index = slot - (lag_down if way else lag_up)
            comes = z < chips - 1 if way else z > 0
            first = 0 if way else chips - 1

            over = index - pieces
            rank = jnp.where(over < 0, 0, 1 + (over // chips) % middles)
            dest = rank if way else chips - 1 - rank
            tile = jnp.where(over < 0, (first + index // 2) % chips, over % chips)
            part = jnp.where(over < 0, index % 2, (over >= items).astype(jnp.int32))
            reaches = dest <= z if way else dest >= z
            sends = dest < z if way else dest > z
            live = jnp.logical_and(index >= 0, over < 2 * items)

            beside = z == (chips - 2 if way else 1)
            opens = jnp.logical_and(index == 0, beside)

            @pl.when(opens)
            def _():
                raw_copy(0).wait_recv()
                raw_copy(1).wait_recv()
                chain_copy(way, dest, tile, part, rest).wait_recv()
                sums[dest, core, tile, part, :raw_rows] = (
                    sums[dest, core, tile, part, :raw_rows] + raw_in[0] + raw_in[1]
                )
                sums[dest, core, tile, part, raw_rows:] = (
                    sums[dest, core, tile, part, raw_rows:]
                    + arrived[dest + 1 - way, tile, part, raw_rows:]
                )

            live = jnp.logical_and(jnp.logical_and(live, comes), reaches)

            @pl.when(jnp.logical_and(live, jnp.logical_not(opens)))
            def _():
                chain_copy(way, dest, tile, part).wait_recv()
                sums[dest, core, tile, part] = (
                    sums[dest, core, tile, part] + arrived[dest + 1 - way, tile, part]
                )

            @pl.when(jnp.logical_and(live, sends))
            def _():
                chain_copy(way, dest, tile, part).start()

        settled = slot - finish_back

        @pl.when(
            jnp.logical_and(jnp.logical_not(is_end), jnp.logical_and(settled >= 0, settled < chips))
        )
        def _():
            columns = pl.ds(pl.multiple_of(settled * wide, wide), wide)
            out_ref[0, half_rows:, columns] = sums[z, core, settled, 1]

        def own_stage(slots_ago, act):
            done = slot - finish - slots_ago

            @pl.when(jnp.logical_and(done >= 0, done < own_count))
            def _():
                tile = jnp.where(is_end, (z + done // 2) % chips, done)
                act(tile, jnp.where(is_end, done % 2, 0), items + done)

        def own_start(tile, part, at):
            first_own(tile, part, at).start()

        def own_mix(tile, part, at):
            first_own(tile, part, at).wait_recv()
            cross_mix(sums[z, core, tile, part], at)

        def own_take(tile, part, at):
            second_copy(at).wait_recv()
            cross_take(mixed[at] + second_in[at], 1 + part, tile)

            @pl.when(at - items >= own_count - jnp.where(is_end, 2, 1))
            def _():
                some = pl.ds(pl.multiple_of(part * half_rows, half_rows), half_rows)

                def store(block, total):
                    out_ref[0, some, block * cb : (block + 1) * cb] = total

                apply_factor(1 + part, store)

        own_stage(0, own_start)

        crossing = slot - item_wait - CROSS_LAG

        @pl.when(jnp.logical_and(crossing >= 0, crossing < items))
        def _():
            dest, tile = item_place(crossing)
            first_item(dest, tile, crossing).wait_recv()
            cross_mix(sums[dest, core, tile, 1], crossing)

        ready = crossing - CROSS_LAG

        @pl.when(jnp.logical_and(ready >= 0, ready < items))
        def _():
            dest, tile = item_place(ready)
            second_copy(ready).wait_recv()
            cross_take(mixed[ready] + second_in[ready], 0, tile)

            @pl.when(tile == chips - 1)
            def _():
                sent(first_in.at[pl.ds(0, chips)], cross_send.at[ready // chips]).wait_send()

                def store(block, total):
                    k = block % per_tile
                    sums[dest, core, block // per_tile, 1, :, k * cb : (k + 1) * cb] = total

                apply_factor(0, store)
                for step in range(chips):
                    end_send(dest, step, 1)

        own_stage(CROSS_LAG, own_mix)
        own_stage(2 * CROSS_LAG, own_take)

        @pl.when(jnp.logical_and(jnp.logical_not(is_end), slot == total - 2))
        def _():
            close()

        return carry

    lax.fori_loop(0, total, slot_step, 0)

    @pl.when(is_end)
    def _():
        close()


def kernel_form(
    pair_devices,
    three_center,
    green_occ,
    green_vir,
    pair_list,
    block_counts,
    cosine_weights,
    coulomb_rows,
    coulomb_blocks,
):
    slots, width, panel = three_center.shape
    chips = pair_devices // 2
    rows = panel // pair_devices
    wide = panel // chips
    piece = (rows // 2, wide)
    blocks, per_block, cb, _ = coulomb_blocks.shape
    normalizer = 1.0 / math.sqrt(slots * width * pair_devices)
    vmem = pl.BlockSpec(memory_space=pltpu.VMEM)
    hbm = pl.BlockSpec(memory_space=pltpu.HBM)
    across = 2 * chips + (chips - 2) * chips
    return pl.pallas_call(
        functools.partial(kernel, chips, normalizer),
        out_shape=pltpu.VMEM((1, rows, panel), jnp.float32),
        in_specs=[hbm] * 8,
        out_specs=vmem,
        scratch_shapes=[
            pltpu.SMEM(pair_list.shape, jnp.int32),
            pltpu.SMEM(block_counts.shape, jnp.int32),
            pltpu.SMEM(cosine_weights.shape, jnp.float32),
            pltpu.SMEM(coulomb_rows.shape[::-1], jnp.int32),
            pltpu.VMEM((chips, slots, width, wide), jnp.bfloat16),
            pltpu.VMEM(green_occ.shape, jnp.bfloat16),
            pltpu.VMEM(green_vir.shape, jnp.bfloat16),
            pltpu.VMEM(coulomb_blocks.shape, jnp.float32),
            pltpu.VMEM((chips, wide, slots * width), jnp.bfloat16),
            pltpu.VMEM((chips, slots * width, wide), jnp.bfloat16),
            pltpu.VMEM((chips, chips, 2) + piece, jnp.float32),
            pltpu.VMEM((chips, 2, chips, 2) + piece, jnp.float32),
            pltpu.VMEM((chips + 1, chips, 2) + piece, jnp.float32),
            pltpu.VMEM((2, 5 * rows // 16, wide), jnp.float32),
            pltpu.VMEM((2, 5 * rows // 16, wide), jnp.float32),
            pltpu.VMEM((across,) + piece, jnp.float32),
            pltpu.VMEM((across,) + piece, jnp.float32),
            pltpu.VMEM((across,) + piece, jnp.float32),
            pltpu.VMEM((across,) + piece, jnp.float32),
            pltpu.VMEM((3, blocks, rows // 2, cb), jnp.float32),
            pltpu.VMEM((blocks, per_block * cb, cb), jnp.bfloat16),
            pltpu.VMEM((blocks, per_block * cb, cb), jnp.bfloat16),
            pltpu.SemaphoreType.DMA((chips,)),
            pltpu.SemaphoreType.DMA((7,)),
            pltpu.SemaphoreType.DMA,
            pltpu.SemaphoreType.DMA((2 * chips - 1,)),
            pltpu.SemaphoreType.DMA,
            pltpu.SemaphoreType.DMA(((chips + 1) * 2 * chips,)),
            pltpu.SemaphoreType.DMA,
            pltpu.SemaphoreType.DMA((2,)),
            pltpu.SemaphoreType.DMA((chips,)),
            pltpu.SemaphoreType.DMA((2, across)),
        ],
        compiler_params=pltpu.CompilerParams(
            collective_id=0, has_side_effects=True, vmem_limit_bytes=60 * 1024 * 1024
        ),
    )(
        pair_list,
        block_counts,
        cosine_weights,
        coulomb_rows.T,
        three_center,
        green_occ,
        green_vir,
        coulomb_blocks,
    )


def solution(mesh):
    times, pair_devices = mesh.shape["tm"], mesh.shape["pair"]

    def local(*args):
        slots, _, panel = args[0].shape
        cb = args[7].shape[2]
        short = 8 <= pair_devices <= 16 and pair_devices % 2 == 0 and times == 4
        fits = panel % (128 * pair_devices) == 0 and cb % 128 == 0 and slots % 2 == 0
        if short and fits and slots <= 32 and (2 * panel // pair_devices) % cb == 0:
            return kernel_form(pair_devices, *args)
        return collective_form(*args)

    return jax.shard_map(
        local,
        mesh=mesh,
        in_specs=(
            P("pair", None, None),
            P("tm", None, None, None),
            P("tm", None, None, None),
            P("pair"),
            P("pair"),
            P(),
            P(),
            P(),
        ),
        out_specs=P("tm", "pair", None),
        check_vma=False,
    )
```
